32 devices in a mesh: ep: 8 (over z, x), tp: 4 (over y, core).
Axes of the slice: x: 2, y: 2, z: 4, core: 2. Of those that a mesh axis runs over, the one named last changes fastest.
Arguments:
- tokens: bfloat16 [1024, 1024], P('ep'), may hold values from -6 to 6
- segment_ids: int32 [8, 128], P('ep'), may hold values from 0 to 15, never falling along the last dimension, each value on 1 to 64 neighbouring positions
- route_ids: int32 [1024, 8], P('ep'), may hold values from 0 to 31, all different within a row; in each aligned block of 128 rows (0 to 127, 128 to 255, ...) at most 64 rows name the same one
- route_weights: float32 [1024, 8], P('ep'), may hold values from 0.03 to 0.3
- attn_gain: bfloat16 [1024], P('ep'), may hold values from 0.099609375 to 1.8984375
- query_weight: bfloat16 [1024, 1024], P('ep', 'tp'), may hold values from -0.1875 to 0.1875
- key_projection_matrix: bfloat16 [1024, 512], P('ep', 'tp'), may hold values from -0.1875 to 0.1875
- value_projection_matrix: bfloat16 [1024, 512], P('ep', 'tp'), may hold values from -0.1875 to 0.1875
- out_weight: bfloat16 [1024, 1024], P('ep', 'tp'), may hold values from -0.75 to 0.75
- ffn_gain: bfloat16 [1024], P('ep'), may hold values from 0.099609375 to 1.8984375
- gate_weight: bfloat16 [32, 1024, 512], P('ep', None, 'tp'), may hold values from -0.1875 to 0.1875
- up_weight: bfloat16 [32, 1024, 512], P('ep', None, 'tp'), may hold values from -0.1875 to 0.1875
- down_weight: bfloat16 [32, 512, 1024], P('ep', 'tp'), may hold values from -0.5 to 0.5
- cotangent: bfloat16 [1024, 1024], P('ep'), may hold values from -6 to 6
Outputs:
- mixed: bfloat16 [1024, 1024], P('ep')
- tokens_grad: float32 [1024, 1024], P('ep')
- attn_gain_grad: float32 [1024], P('ep')
- query_grad: float32 [1024, 1024], P('ep', 'tp')
- key_grad: float32 [1024, 512], P('ep', 'tp')
- value_grad: float32 [1024, 512], P('ep', 'tp')
- out_grad: float32 [1024, 1024], P('ep', 'tp')
- ffn_gain_grad: float32 [1024], P('ep')
- gate_grad: float32 [32, 1024, 512], P('ep', None, 'tp')
- up_grad: float32 [32, 1024, 512], P('ep', None, 'tp')
- down_grad: float32 [32, 512, 1024], P('ep', 'tp')
The draws below stay inside these ranges and needn't reach their ends.
Inputs may be any that keep to these rules, and one draw needn't show every extreme that they name: `segment_ids`: each row is non-decreasing; every sequence has 1 to 64 tokens and some sequence has exactly 64. `route_ids`: the 8 experts of a token differ; among the rows of one ep group no expert is named more than 64 times, and in some group some expert exactly 64 times.
All inputs are finite; a program needn't handle non-finite values.
Results may differ from the reference program's by a relative error of at most 0.012.
Values may be sent and summed in bfloat16 or wider, within the bound.
No kernel may reach another device: no remote copies, remote signals or barrier semaphores. Data moves between devices by JAX's collectives and lax.ppermute only.
A program may use at most 128 MiB of HBM per device.

```python
import math
import jax
import jax.numpy as jnp
import numpy as np
from jax import lax

MODEL_WIDTH = 1024
HQ = 16
KEY_VALUE_HEADS = 8
HEAD_SIZE = 64
EXPERTS = 32
FF = 512
TOP = 8
TOK_DEV = 128
MAX_LEN = 64
CAP = 64
TOKENS = 1024
N_EP = 8
N_TP = 4


def block_scale(key, extent, shards, smallest, largest):
    level = 1.0
    for axis_at, parts in shards:
        steps = jax.random.uniform(jax.random.fold_in(jax.random.fold_in(key, 6), axis_at), (parts,), jnp.float32, smallest / len(shards), largest / len(shards))
        level = level * jnp.repeat(jnp.exp(steps), extent[axis_at] // parts).reshape((-1,) + (1,) * (len(extent) - 1 - axis_at))
    return level


def profile(amount, total, bound, lean):
    portions = [(1 << 20) // math.isqrt(standing ** lean) + 1 for standing in range(2, amount + 1)]
    spare, given = total - bound - (amount - 1), [1] * (amount - 1)
    while spare > 0:
        movable = [i for i in range(amount - 1) if given[i] < bound]
        pool, budget = sum([portions[i] for i in movable]), spare
        for i in movable:
            addition = min(bound - given[i], max(1, budget * portions[i] // pool), spare)
            given[i] = given[i] + addition
            spare = spare - addition
    return np.array([bound] + given)


def ragged(rng, count, total, most, slope):
    if count == 2:
        one = jax.random.randint(rng, (), max(1, total - most), min(most, total - 1) + 1)
        return jnp.stack([one, total - one])
    lengths = jnp.asarray(profile(count, total, most, slope), jnp.int32)
    pairs = (count - 1) // 2
    giver, receiver = lengths[1:1 + 2 * pairs:2], lengths[2:2 + 2 * pairs:2]
    slack = jnp.minimum(giver - 1, most - receiver)
    passed = jax.random.randint(jax.random.fold_in(rng, 1), (pairs,), 0, 1 << 20) % (slack + 1)
    lengths = lengths.at[1:1 + 2 * pairs:2].set(giver - passed).at[2:2 + 2 * pairs:2].set(receiver + passed)
    return lengths[jax.random.permutation(jax.random.fold_in(rng, 2), count)]


def routed_block(key, own, number, rows, count, top, most, lean):
    order = jax.random.permutation(key, count)
    heavy_load, ordinary = shares(count, rows * top, most, lean, True), shares(count, rows * top, most, lean, False)
    places = jnp.arange(count)

    def named(tallies, turn):
        used = int((tallies > 0).sum())
        fixed = max(1, used // 4)
        shifted = fixed + (places - fixed + turn * (used - fixed)) % max(1, count - fixed)
        return jnp.zeros((count,), jnp.int32).at[order[jnp.where(places < fixed, places, shifted)]].set(jnp.asarray(tallies, jnp.int32))

    tallies = jnp.where(number % 4 == 0, named(heavy_load, number // 4), named(ordinary, number - number // 4 - 1))
    mixed = jax.random.permutation(jax.random.fold_in(own, 3), count)
    donor, taker = mixed[0:count // 2 * 2:2], mixed[1:count // 2 * 2:2]
    room = jnp.minimum(tallies[donor] - 1, most - tallies[taker]) // 2
    room = jnp.where((donor == order[0]) | (taker == order[0]) | (tallies[taker] == 0), 0, jnp.maximum(room, 0))
    shifted = jax.random.randint(jax.random.fold_in(own, 4), (count // 2,), 0, 1 << 20) % (room + 1)
    tallies = tallies.at[donor].add(-shifted).at[taker].add(shifted)
    members = jnp.searchsorted(jnp.cumsum(tallies), jnp.arange(rows * top), side="right").astype(jnp.int32)
    grid = members.reshape(top, rows).T
    grid = grid[jax.random.permutation(jax.random.fold_in(own, 1), rows)]
    turn = jax.random.randint(jax.random.fold_in(own, 2), (rows, 1), 0, top)
    return jnp.take_along_axis(grid, (jnp.arange(top)[None, :] + turn) % top, axis=1)


def shares(count, total, most, slope, full):
    weights = [(1 << 20) // math.isqrt(rank ** slope) + 1 for rank in range(1, count + 1)]
    largest = most if full else min(most, max(-(-total // count), total * weights[0] // sum(weights)))
    least = 1 if total - largest >= count - 1 else 0
    counts, spare = [largest] + [least] * (count - 1), total - largest - least * (count - 1)
    while spare > 0:
        free = [i for i in range(1, count) if counts[i] < largest] or [i for i in range(1, count) if counts[i] < most]
        mass, budget = sum([weights[i] for i in free]), spare
        for i in free:
            extra = min(most - counts[i], max(1, budget * weights[i] // mass), spare)
            counts[i] = counts[i] + extra
            spare = spare - extra
    return np.array(counts)


def scatter_about(own_key, shape, scale, most, shards=(), kind=jnp.bfloat16):
    drawn = jax.random.normal(own_key, shape, jnp.float32) * scale
    if len(shards) > 0:
        drawn = block_scale(own_key, shape, shards, -0.22, 0.18) * drawn
    return jnp.clip(drawn, min=-most, max=most).astype(kind)


def setup_inputs(seed: int = 0) -> dict:
    key_list = jax.random.split(jax.random.key(seed), 15)
    tokens = scatter_about(key_list[0], (TOKENS, MODEL_WIDTH), 1.0, 6.0, ((0, 8),))
    segment_ids = jax.vmap(lambda own: jnp.searchsorted(jnp.cumsum(ragged(own, TOK_DEV // 8, TOK_DEV, MAX_LEN, 2)), jnp.arange(TOK_DEV), side="right"))(jax.random.split(key_list[1], N_EP)).reshape((N_EP, TOK_DEV)).astype(jnp.int32)
    route_ids_keys = jax.random.split(jax.random.fold_in(key_list[2], 1), TOKENS // TOK_DEV)
    route_ids_turns = jax.random.permutation(jax.random.fold_in(key_list[2], 3), TOKENS // TOK_DEV)
    route_ids = jax.vmap(lambda own, number: routed_block(jax.random.fold_in(key_list[2], 2), own, number, TOK_DEV, EXPERTS, TOP, CAP, 2))(route_ids_keys, route_ids_turns).reshape((TOKENS, TOP))
    route_weights = jnp.clip(0.03 + 0.27 * jax.random.uniform(key_list[3], (TOKENS, TOP), jnp.float32) ** block_scale(key_list[3], (TOKENS, TOP), ((0, 8),), -0.2, 0.2), 0.03, 0.3)
    attn_gain = jnp.clip(1.0 + 0.18 * jax.random.normal(key_list[4], (MODEL_WIDTH,), jnp.float32), 0.099609375, 1.8984375).astype(jnp.bfloat16)
    query_weight = scatter_about(key_list[5], (MODEL_WIDTH, HQ * HEAD_SIZE), MODEL_WIDTH ** -0.5, 0.1875, ((0, 8), (1, 4)))
    key_projection_matrix = scatter_about(key_list[6], (MODEL_WIDTH, KEY_VALUE_HEADS * HEAD_SIZE), MODEL_WIDTH ** -0.5, 0.1875, ((0, 8), (1, 4)))
    value_projection_matrix = scatter_about(key_list[7], (MODEL_WIDTH, KEY_VALUE_HEADS * HEAD_SIZE), MODEL_WIDTH ** -0.5, 0.1875, ((0, 8), (1, 4)))
    out_weight = scatter_about(key_list[8], (MODEL_WIDTH, HQ * HEAD_SIZE), HEAD_SIZE ** -0.5, 0.75, ((0, 8), (1, 4)))
    ffn_gain = jnp.clip(1.0 + 0.18 * jax.random.normal(key_list[9], (MODEL_WIDTH,), jnp.float32), 0.099609375, 1.8984375).astype(jnp.bfloat16)
    gate_weight = scatter_about(key_list[10], (EXPERTS, MODEL_WIDTH, FF), MODEL_WIDTH ** -0.5, 0.1875, ((0, 8), (2, 4)))
    up_weight = scatter_about(key_list[11], (EXPERTS, MODEL_WIDTH, FF), MODEL_WIDTH ** -0.5, 0.1875, ((0, 8), (2, 4)))
    down_weight = scatter_about(key_list[12], (EXPERTS, FF, MODEL_WIDTH), (FF // 4) ** -0.5, 0.5, ((0, 8), (1, 4)))
    cotangent = scatter_about(key_list[13], (TOKENS, MODEL_WIDTH), 1.0, 6.0, ((0, 8),))
    return dict(tokens=tokens, segment_ids=segment_ids, route_ids=route_ids, route_weights=route_weights, attn_gain=attn_gain, query_weight=query_weight, key_projection_matrix=key_projection_matrix, value_projection_matrix=value_projection_matrix, out_weight=out_weight, ffn_gain=ffn_gain, gate_weight=gate_weight, up_weight=up_weight, down_weight=down_weight, cotangent=cotangent)


NORM_EPSILON = 1e-06
ROPE_BASE = 10000.0
MASKED = -1e+30

def widen(values):
    return lax.optimization_barrier(values).astype(jnp.float32)

def positions_and_mask(segment_row):
    count = segment_row.shape[0]
    index = jnp.arange(count, dtype=jnp.int32)
    same = segment_row[:, None] == segment_row[None, :]
    before = index[None, :] < index[:, None]
    position = lax.optimization_barrier(jnp.sum((same & before).astype(jnp.int32), axis=1))
    allowed = same & (index[None, :] <= index[:, None])
    return (position, allowed)

def rope_tables(position):
    half = HEAD_SIZE // 2
    steps = jnp.arange(half, dtype=jnp.float32) * (2.0 / HEAD_SIZE)
    frequency = jnp.exp(-jnp.log(jnp.float32(ROPE_BASE)) * steps)
    angle = position.astype(jnp.float32)[:, None] * frequency[None, :]
    return (jnp.cos(angle)[:, None, :], jnp.sin(angle)[:, None, :])

def rotate(values, cosine, sine):
    half = values.shape[-1] // 2
    first = values[..., :half]
    second = values[..., half:]
    return jnp.concatenate([first * cosine - second * sine, second * cosine + first * sine], axis=-1)

def rotate_back(values, cosine, sine):
    half = values.shape[-1] // 2
    first = values[..., :half]
    second = values[..., half:]
    return jnp.concatenate([first * cosine + second * sine, second * cosine - first * sine], axis=-1)

def rms_inverse(values):
    return lax.rsqrt(lax.optimization_barrier(jnp.mean(values * values, axis=-1, keepdims=True)) + NORM_EPSILON)

def rms_backward(values, inverse, gain, upstream):
    gain_term = lax.optimization_barrier(jnp.sum(upstream * values * inverse, axis=0))
    inner = lax.optimization_barrier(jnp.mean(values * gain * upstream, axis=-1, keepdims=True))
    input_term = inverse * (gain * upstream) - values * inverse * inverse * inverse * inner
    return (input_term, gain_term)

def dispatch_table(route_rows):
    flat = route_rows.reshape(-1)
    onehot = (flat[:, None] == jnp.arange(EXPERTS, dtype=jnp.int32)[None, :]).astype(jnp.int32)
    before = jnp.cumsum(onehot, axis=0) - onehot
    slot = lax.optimization_barrier(jnp.sum(before * onehot, axis=1))
    dest = (flat * CAP + slot).astype(jnp.int32)
    table = jnp.full((EXPERTS * CAP,), -1, jnp.int32).at[dest].set(jnp.arange(flat.shape[0], dtype=jnp.int32))
    return (dest, table)

def attend(grouped, key_rot, value_rows, allowed, scale):
    scores = jnp.einsum('thgd,uhd->hgtu', widen(grouped), widen(key_rot)) * scale
    scores = jnp.where(allowed, scores, MASKED)
    peak = lax.optimization_barrier(jnp.max(scores, axis=-1, keepdims=True))
    logsum = peak[..., 0] + jnp.log(lax.optimization_barrier(jnp.sum(jnp.exp(scores - peak), axis=-1)))
    probs = jnp.exp(scores - logsum[..., None]).astype(jnp.bfloat16)
    attended = jnp.einsum('hgtu,uhd->thgd', widen(probs), widen(value_rows)).astype(jnp.bfloat16)
    return (attended, logsum)

def attend_back(grouped, key_rot, value_rows, attended, logsum, grad_attended, allowed, scale):
    scores = jnp.einsum('thgd,uhd->hgtu', widen(grouped), widen(key_rot)) * scale
    scores = jnp.where(allowed, scores, MASKED)
    probs = jnp.exp(scores - logsum[..., None])
    probs_low = probs.astype(jnp.bfloat16)
    value_grad = jnp.einsum('hgtu,thgd->uhd', widen(probs_low), widen(grad_attended))
    grad_probs = jnp.einsum('thgd,uhd->hgtu', widen(grad_attended), widen(value_rows))
    delta = jnp.einsum('thgd,thgd->hgt', widen(grad_attended), widen(attended))
    grad_scores = (probs * (grad_probs - delta[..., None]) * scale).astype(jnp.bfloat16)
    query_grad = jnp.einsum('hgtu,uhd->thgd', widen(grad_scores), widen(key_rot))
    key_grad = jnp.einsum('hgtu,thgd->uhd', widen(grad_scores), widen(grouped))
    return (query_grad, key_grad, value_grad)

def reference(tokens, segment_ids, route_ids, route_weights, attn_gain, query_weight, key_projection_matrix, value_projection_matrix, out_weight, ffn_gain, gate_weight, up_weight, down_weight, cotangent):
    scale = HEAD_SIZE ** (-0.5)
    gain_one = attn_gain.astype(jnp.float32)
    second_norm_gain = ffn_gain.astype(jnp.float32)
    width = tokens.shape[1]

    def front(inputs):
        group_rows, segment_row = inputs
        position, allowed = positions_and_mask(segment_row)
        cosine, sine = rope_tables(position)
        rows = group_rows.shape[0]
        tokens_float = group_rows.astype(jnp.float32)
        inverse_one = rms_inverse(tokens_float)
        normed_one = (tokens_float * inverse_one * gain_one).astype(jnp.bfloat16)
        query = jnp.dot(normed_one, query_weight, preferred_element_type=jnp.float32).reshape(rows, -1, HEAD_SIZE)
        keys = jnp.dot(normed_one, key_projection_matrix, preferred_element_type=jnp.float32).reshape(rows, -1, HEAD_SIZE)
        query_rot = rotate(query, cosine, sine).astype(jnp.bfloat16)
        key_rot = rotate(keys, cosine, sine).astype(jnp.bfloat16)
        value_rows = jnp.dot(normed_one, value_projection_matrix, preferred_element_type=jnp.float32).astype(jnp.bfloat16).reshape(rows, -1, HEAD_SIZE)
        grouped = query_rot.reshape(rows, key_rot.shape[1], -1, HEAD_SIZE)
        attended, logsum = attend(grouped, key_rot, value_rows, allowed, scale)
        attended_flat = attended.reshape(rows, -1)
        branch = jnp.dot(attended_flat, out_weight.T, preferred_element_type=jnp.float32)
        hidden_one = tokens_float + branch
        inverse_two = rms_inverse(hidden_one)
        normed_two = (hidden_one * inverse_two * second_norm_gain).astype(jnp.bfloat16)
        return (hidden_one, normed_one, normed_two, grouped, key_rot, value_rows, attended, logsum, inverse_one, inverse_two)
    grouped_tokens = tokens.reshape(N_EP, TOK_DEV, width)
    fronts = lax.map(front, (grouped_tokens, segment_ids))
    hidden_one, normed_one, normed_two, grouped, key_rot, value_rows, attended, logsum, inverse_one, inverse_two = fronts
    dest_all, table_all = lax.map(dispatch_table, route_ids.reshape(N_EP, TOK_DEV, TOP))
    valid = table_all >= 0
    source = jnp.maximum(table_all, 0)
    offsets = (jnp.arange(N_EP, dtype=jnp.int32) * TOK_DEV)[:, None]
    token_global = source // TOP + offsets
    flat_weights = route_weights.reshape(N_EP, TOK_DEV * TOP)
    slot_weight = jnp.where(valid, jnp.take_along_axis(flat_weights, source, axis=1), 0.0)
    normed_two_all = normed_two.reshape(-1, width)
    sends = jnp.where(valid[..., None], normed_two_all[token_global], jnp.zeros((), jnp.bfloat16))
    grad_rows = (cotangent[token_global].astype(jnp.float32) * slot_weight[..., None]).astype(jnp.bfloat16)

    def by_expert(values):
        rest = values.shape[2:]
        return values.reshape((N_EP, EXPERTS, CAP) + rest).swapaxes(0, 1).reshape((EXPERTS, N_EP * CAP) + rest)
    block = FF // N_TP

    def expert_step(carry, inputs):
        branch_sum, grad_sum = carry
        rows_in, grad_in_rows, token_index, weight_index, gate_mat, up_mat, down_mat = inputs
        count = rows_in.shape[0]
        gate_pre = jnp.dot(rows_in, gate_mat, preferred_element_type=jnp.float32)
        up_pre = jnp.dot(rows_in, up_mat, preferred_element_type=jnp.float32)
        sigma = jax.nn.sigmoid(gate_pre)
        active = gate_pre * sigma
        hidden = (active * up_pre).astype(jnp.bfloat16)
        expert_out = jnp.einsum('rjf,jfd->rjd', widen(hidden).reshape(count, N_TP, block), widen(down_mat).reshape(N_TP, block, width)).astype(jnp.bfloat16)
        out_total = lax.optimization_barrier(jnp.sum(widen(expert_out), axis=1))
        branch_sum = branch_sum.at[token_index].add(weight_index[:, None] * out_total)
        grad_hidden = jnp.dot(grad_in_rows, down_mat.T, preferred_element_type=jnp.float32)
        down_part = jnp.dot(hidden.T, grad_in_rows, preferred_element_type=jnp.float32)
        grad_gate = (grad_hidden * up_pre * sigma * (1.0 + gate_pre * (1.0 - sigma))).astype(jnp.bfloat16)
        grad_up = (grad_hidden * active).astype(jnp.bfloat16)
        gate_part = jnp.dot(rows_in.T, grad_gate, preferred_element_type=jnp.float32)
        up_part = jnp.dot(rows_in.T, grad_up, preferred_element_type=jnp.float32)
        back_gate = jnp.einsum('rjf,djf->rjd', widen(grad_gate).reshape(count, N_TP, block), widen(gate_mat).reshape(width, N_TP, block))
        back_up = jnp.einsum('rjf,djf->rjd', widen(grad_up).reshape(count, N_TP, block), widen(up_mat).reshape(width, N_TP, block))
        grad_in = (back_gate + back_up).astype(jnp.bfloat16)
        grad_sum = grad_sum.at[token_index].add(lax.optimization_barrier(jnp.sum(widen(grad_in), axis=1)))
        return ((branch_sum, grad_sum), (gate_part, up_part, down_part))
    zeros_rows = jnp.zeros((N_EP * TOK_DEV, width), jnp.float32)
    carry, expert_grads = lax.scan(expert_step, (zeros_rows, zeros_rows), (by_expert(sends), by_expert(grad_rows), by_expert(token_global), by_expert(slot_weight), gate_weight, up_weight, down_weight))
    branch_moe, grad_normed_two = carry
    gate_grad, up_grad, down_grad = expert_grads
    hidden_all = hidden_one.reshape(-1, width)
    inverse_two_all = inverse_two.reshape(-1, 1)
    mixed = (hidden_all + branch_moe).astype(jnp.bfloat16)
    grad_out = cotangent.astype(jnp.float32)
    norm_term, ffn_gain_grad = rms_backward(hidden_all, inverse_two_all, second_norm_gain, grad_normed_two)
    grad_hidden_one = grad_out + norm_term

    def back_group(carry, inputs):
        query_acc, key_acc, value_acc, out_acc = carry
        grad_group, normed_group, grouped_group, key_group, value_group, attended_group, logsum_group, segment_row = inputs
        position, allowed = positions_and_mask(segment_row)
        cosine, sine = rope_tables(position)
        rows = grad_group.shape[0]
        grad_branch = grad_group.astype(jnp.bfloat16)
        attended_flat = attended_group.reshape(rows, -1)
        out_part = jnp.dot(grad_branch.T, attended_flat, preferred_element_type=jnp.float32)
        grad_attended = jnp.dot(grad_branch, out_weight, preferred_element_type=jnp.float32).astype(jnp.bfloat16)
        grad_attended = grad_attended.reshape(attended_group.shape)
        query_grad_rot, key_grad_rot, value_grad_rows = attend_back(grouped_group, key_group, value_group, attended_group, logsum_group, grad_attended, allowed, scale)
        query_grad_rows = rotate_back(query_grad_rot.reshape(rows, -1, HEAD_SIZE), cosine, sine).astype(jnp.bfloat16).reshape(rows, -1)
        key_grad_rows = rotate_back(key_grad_rot, cosine, sine).astype(jnp.bfloat16).reshape(rows, -1)
        value_low = value_grad_rows.astype(jnp.bfloat16).reshape(rows, -1)
        grad_normed_one = jnp.dot(query_grad_rows, query_weight.T, preferred_element_type=jnp.float32)
        grad_normed_one = grad_normed_one + jnp.dot(key_grad_rows, key_projection_matrix.T, preferred_element_type=jnp.float32)
        grad_normed_one = grad_normed_one + jnp.dot(value_low, value_projection_matrix.T, preferred_element_type=jnp.float32)
        query_acc = query_acc + jnp.dot(normed_group.T, query_grad_rows, preferred_element_type=jnp.float32)
        key_acc = key_acc + jnp.dot(normed_group.T, key_grad_rows, preferred_element_type=jnp.float32)
        value_acc = value_acc + jnp.dot(normed_group.T, value_low, preferred_element_type=jnp.float32)
        out_acc = out_acc + out_part
        return ((query_acc, key_acc, value_acc, out_acc), grad_normed_one)
    start = (jnp.zeros(query_weight.shape, jnp.float32), jnp.zeros(key_projection_matrix.shape, jnp.float32), jnp.zeros(value_projection_matrix.shape, jnp.float32), jnp.zeros(out_weight.shape, jnp.float32))
    grads, grad_normed_one = lax.scan(back_group, start, (grad_hidden_one.reshape(N_EP, TOK_DEV, width), normed_one, grouped, key_rot, value_rows, attended, logsum, segment_ids))
    query_grad, key_grad, value_grad, out_grad = grads
    tokens_float = tokens.astype(jnp.float32)
    input_term, attn_gain_grad = rms_backward(tokens_float, inverse_one.reshape(-1, 1), gain_one, grad_normed_one.reshape(-1, width))
    tokens_grad = grad_hidden_one + input_term
    return (mixed, tokens_grad, attn_gain_grad, query_grad, key_grad, value_grad, out_grad, ffn_gain_grad, gate_grad, up_grad, down_grad)
```

```python
import jax
import jax.numpy as jnp
from jax import lax
from jax.sharding import PartitionSpec as P

HEAD_SIZE = 64
NORM_EPSILON = 1e-06
ROPE_BASE = 10000.0
MASKED = -1e30
LANES = 128
SUBLANES = 16
bf16 = jnp.bfloat16
f32 = jnp.float32


def positions_and_mask(segment_row):
    count = segment_row.shape[0]
    index = jnp.arange(count, dtype=jnp.int32)
    same = segment_row[:, None] == segment_row[None, :]
    before = index[None, :] < index[:, None]
    position = jnp.sum((same & before).astype(jnp.int32), axis=1)
    allowed = same & (index[None, :] <= index[:, None])
    return (position, allowed)


def rope_tables(position):
    half = HEAD_SIZE // 2
    steps = jnp.arange(half, dtype=f32) * (2.0 / HEAD_SIZE)
    frequency = jnp.exp(-jnp.log(f32(ROPE_BASE)) * steps)
    angle = position.astype(f32)[:, None] * frequency[None, :]
    return (jnp.cos(angle)[:, None, :], jnp.sin(angle)[:, None, :])


def rotate(values, cosine, sine):
    half = values.shape[-1] // 2
    first = values[..., :half]
    second = values[..., half:]
    return jnp.concatenate(
        [first * cosine - second * sine, second * cosine + first * sine], axis=-1
    )


def rotate_back(values, cosine, sine):
    return rotate(values, cosine, -sine)


def rms_inverse(values):
    return lax.rsqrt(jnp.mean(values * values, axis=-1, keepdims=True) + NORM_EPSILON)


def rms_backward(values, inverse, gain, upstream):
    gain_term = jnp.sum(upstream * values * inverse, axis=0)
    inner = jnp.mean(values * gain * upstream, axis=-1, keepdims=True)
    input_term = inverse * (gain * upstream) - values * inverse * inverse * inverse * inner
    return (input_term, gain_term)


def exchange(blocks, axis):
    return lax.all_to_all(blocks, axis, split_axis=0, concat_axis=0, tiled=True)


def gather_blocks(value, axis):
    count = lax.axis_size(axis)
    return exchange(jnp.broadcast_to(value[None], (count,) + value.shape), axis)


def flip(value, axis, bit):
    count = lax.axis_size(axis)
    return lax.ppermute(value, axis, [(i, i ^ bit) for i in range(count)])


def bits_of(axis):
    count = lax.axis_size(axis)
    return [1 << i for i in range(count.bit_length() - 1)]


def gather_relative(value, axis):
    for bit in reversed(bits_of(axis)):
        value = jnp.stack([value, flip(value, axis, bit)])
    return value


def reduce_relative(value, axis):
    for bit in bits_of(axis):
        value = value[0] + flip(value[1].astype(bf16), axis, bit).astype(f32)
    return value


def split_pair(value):
    high = lax.reduce_precision(value, 8, 7)
    return (high.astype(bf16), (value - high).astype(bf16))


def pad_to(value, axis, size):
    widths = [(0, 0)] * value.ndim
    widths[axis] = (0, size - value.shape[axis])
    return jnp.pad(value, widths)


def body(
    tokens,
    segment_ids,
    route_ids,
    route_weights,
    attn_gain,
    query_weight,
    key_projection_matrix,
    value_projection_matrix,
    out_weight,
    ffn_gain,
    gate_weight,
    up_weight,
    down_weight,
    cotangent,
):
    n_ep = lax.axis_size("ep")
    n_tp = lax.axis_size("tp")
    tp_at = lax.axis_index("tp")
    rows, width = tokens.shape
    sub = rows // n_tp
    piece = width // n_ep
    local_experts, _, units = gate_weight.shape
    experts = local_experts * n_ep
    total = rows * n_ep
    scale = HEAD_SIZE ** (-0.5)
    q_cols = query_weight.shape[1]
    k_cols = key_projection_matrix.shape[1]

    def own_rows(value):
        return lax.dynamic_slice_in_dim(value, tp_at * sub, sub, 0)

    qkv_shard = jnp.concatenate([query_weight, key_projection_matrix, value_projection_matrix], 1)
    cols = qkv_shard.shape[1]
    gain_rows = pad_to(pad_to(jnp.stack([attn_gain, ffn_gain]), 1, cols), 0, SUBLANES)
    packed = gather_blocks(jnp.concatenate([qkv_shard, gain_rows], 0), "ep")
    qkv_full = packed[:, :piece].reshape(width, cols)
    gain_one = packed[:, piece, :piece].reshape(width).astype(f32)
    gain_two = packed[:, piece + 1, :piece].reshape(width).astype(f32)
    out_full = gather_blocks(out_weight, "ep").reshape(width, -1)

    expert_index = jnp.arange(experts, dtype=jnp.int32)
    own_ids = own_rows(route_ids)
    own_weights = own_rows(route_weights)
    dense = jnp.sum(
        jnp.where(own_ids[:, :, None] == expert_index, own_weights[:, :, None], 0.0), axis=1
    )
    dense = dense.reshape(sub, n_ep, local_experts).swapaxes(0, 1)
    dense_high, dense_low = split_pair(dense)
    dense_pack = pad_to(jnp.concatenate([dense_high, dense_low], -1), 2, LANES)
    cot_own = own_rows(cotangent)
    cot_pack = jnp.concatenate(
        [jnp.broadcast_to(cot_own[None], (n_ep, sub, width)), dense_pack], axis=-1
    )
    cot_all = gather_relative(exchange(cot_pack, "ep"), "tp").reshape(total, -1)
    weights_all = cot_all[:, width : width + local_experts].astype(f32) + cot_all[
        :, width + local_experts : width + 2 * local_experts
    ].astype(f32)
    cot_all = cot_all[:, :width]

    position, allowed = positions_and_mask(segment_ids[0])
    cosine, sine = rope_tables(position)
    tokens_float = tokens.astype(f32)
    inverse_one = rms_inverse(tokens_float)
    normed_one = (tokens_float * inverse_one * gain_one).astype(bf16)
    qkv = jnp.dot(normed_one, qkv_full, preferred_element_type=f32)
    query = qkv[:, :q_cols].reshape(rows, -1, HEAD_SIZE)
    keys = qkv[:, q_cols : q_cols + k_cols].reshape(rows, -1, HEAD_SIZE)
    query_rot = rotate(query, cosine, sine).astype(bf16)
    key_rot = rotate(keys, cosine, sine).astype(bf16)
    value_rows = qkv[:, q_cols + k_cols :].astype(bf16).reshape(rows, -1, HEAD_SIZE)
    grouped = query_rot.reshape(rows, key_rot.shape[1], -1, HEAD_SIZE)
    scores = jnp.einsum("thgd,uhd->hgtu", grouped, key_rot, preferred_element_type=f32) * scale
    scores = jnp.where(allowed, scores, MASKED)
    peak = jnp.max(scores, axis=-1, keepdims=True)
    logsum = peak + jnp.log(jnp.sum(jnp.exp(scores - peak), axis=-1, keepdims=True))
    probs = jnp.exp(scores - logsum)
    probs_low = probs.astype(bf16)
    attended = jnp.einsum(
        "hgtu,uhd->thgd", probs_low, value_rows, preferred_element_type=f32
    ).astype(bf16)
    attended_flat = attended.reshape(rows, -1)
    branch_part = jnp.einsum("tk,dk->td", attended_flat, out_full, preferred_element_type=f32)
    branch = exchange(branch_part.astype(bf16).reshape(n_tp, sub, width), "tp")
    branch = jnp.sum(branch.astype(f32), axis=0)
    tokens_own = own_rows(tokens).astype(f32)
    hidden_one = tokens_own + branch
    inverse_two = rms_inverse(hidden_one)
    normed_two = (hidden_one * inverse_two * gain_two).astype(bf16)

    rows_in = gather_relative(gather_blocks(normed_two, "ep"), "tp").reshape(total, width)
    gate_pre = jnp.einsum("td,edf->tef", rows_in, gate_weight, preferred_element_type=f32)
    up_pre = jnp.einsum("td,edf->tef", rows_in, up_weight, preferred_element_type=f32)
    sigma = jax.nn.sigmoid(gate_pre)
    active = gate_pre * sigma
    route = weights_all[:, :, None]
    hidden = (active * up_pre * route).astype(bf16)
    grad_hidden = (
        jnp.einsum("td,efd->tef", cot_all, down_weight, preferred_element_type=f32) * route
    )
    grad_gate = (grad_hidden * up_pre * sigma * (1.0 + gate_pre * (1.0 - sigma))).astype(bf16)
    grad_up = (grad_hidden * active).astype(bf16)
    grad_in = jnp.einsum("tef,edf->td", grad_gate, gate_weight, preferred_element_type=f32)
    grad_in = grad_in + jnp.einsum("tef,edf->td", grad_up, up_weight, preferred_element_type=f32)
    blocks = (2,) * (n_tp.bit_length() - 1) + (n_ep, sub, width)
    grad_part = reduce_relative(grad_in.reshape(blocks), "tp")
    grad_normed_two = jnp.sum(exchange(grad_part.astype(bf16), "ep").astype(f32), axis=0)

    moe = jnp.einsum("tef,efd->td", hidden, down_weight, preferred_element_type=f32)
    moe_part = reduce_relative(moe.reshape(blocks), "tp")
    moe_own = jnp.sum(exchange(moe_part.astype(bf16), "ep").astype(f32), axis=0)
    mixed = lax.all_gather((hidden_one + moe_own).astype(bf16), "tp", axis=0, tiled=True)
    down_grad = jnp.einsum("tef,td->efd", hidden, cot_all, preferred_element_type=f32)
    gate_grad = jnp.einsum("td,tef->edf", rows_in, grad_gate, preferred_element_type=f32)
    up_grad = jnp.einsum("td,tef->edf", rows_in, grad_up, preferred_element_type=f32)

    norm_term, ffn_gain_part = rms_backward(hidden_one, inverse_two, gain_two, grad_normed_two)
    grad_hidden_one = cot_own.astype(f32) + norm_term
    ffn_rows = pad_to(jnp.stack(split_pair(ffn_gain_part)), 0, SUBLANES)
    branch_rows = lax.all_gather(
        jnp.concatenate([grad_hidden_one.astype(bf16), ffn_rows], 0), "tp", axis=0
    )
    grad_branch = branch_rows[:, :sub].reshape(rows, width)
    ffn_gain_part = jnp.sum(branch_rows[:, sub : sub + 2].astype(f32), axis=(0, 1))

    grad_attended = (
        jnp.dot(grad_branch, out_full, preferred_element_type=f32)
        .astype(bf16)
        .reshape(attended.shape)
    )
    value_grad = jnp.einsum("hgtu,thgd->uhd", probs_low, grad_attended, preferred_element_type=f32)
    grad_probs = jnp.einsum("thgd,uhd->hgtu", grad_attended, value_rows, preferred_element_type=f32)
    delta = jnp.einsum("thgd,thgd->hgt", grad_attended, attended, preferred_element_type=f32)
    grad_scores = (probs * (grad_probs - delta[..., None]) * scale).astype(bf16)
    query_grad_rot = jnp.einsum("hgtu,uhd->thgd", grad_scores, key_rot, preferred_element_type=f32)
    key_grad_rot = jnp.einsum("hgtu,thgd->uhd", grad_scores, grouped, preferred_element_type=f32)
    query_back = rotate_back(query_grad_rot.reshape(rows, -1, HEAD_SIZE), cosine, sine)
    key_back = rotate_back(key_grad_rot, cosine, sine)
    qkv_grad = jnp.concatenate(
        [
            query_back.reshape(rows, -1).astype(bf16),
            key_back.reshape(rows, -1).astype(bf16),
            value_grad.reshape(rows, -1).astype(bf16),
        ],
        axis=1,
    )

    grad_normed_part = jnp.einsum("tk,dk->td", qkv_grad, qkv_full, preferred_element_type=f32)
    grad_normed_one = exchange(grad_normed_part.astype(bf16).reshape(n_tp, sub, width), "tp")
    grad_normed_one = jnp.sum(grad_normed_one.astype(f32), axis=0)
    input_term, attn_gain_part = rms_backward(
        tokens_own, own_rows(inverse_one), gain_one, grad_normed_one
    )
    attn_rows = pad_to(jnp.stack(split_pair(attn_gain_part)), 0, SUBLANES)
    last_rows = lax.all_gather(
        jnp.concatenate([(grad_hidden_one + input_term).astype(bf16), attn_rows], 0), "tp", axis=0
    )
    tokens_grad = last_rows[:, :sub].reshape(rows, width).astype(f32)
    attn_gain_part = jnp.sum(last_rows[:, sub : sub + 2].astype(f32), axis=(0, 1))
    attn_gain_grad = jnp.sum(exchange(attn_gain_part.reshape(n_ep, 1, piece), "ep"), axis=(0, 1))

    def by_piece(value):
        return value.reshape(rows, n_ep, piece).swapaxes(0, 1)

    early = exchange(
        jnp.concatenate(
            [
                jnp.broadcast_to(attended_flat[None], (n_ep,) + attended_flat.shape),
                by_piece(normed_one),
            ],
            axis=-1,
        ),
        "ep",
    ).reshape(total, -1)
    late = jnp.concatenate(
        [jnp.broadcast_to(qkv_grad[None], (n_ep,) + qkv_grad.shape), by_piece(grad_branch)], axis=-1
    )
    ffn_pair = jnp.stack(split_pair(ffn_gain_part)).reshape(2, n_ep, piece).swapaxes(0, 1)
    ffn_pair = pad_to(pad_to(ffn_pair, 2, late.shape[2]), 1, SUBLANES)
    late = exchange(jnp.concatenate([late, ffn_pair], axis=1), "ep")
    ffn_gain_grad = jnp.sum(late[:, rows : rows + 2, :piece].astype(f32), axis=(0, 1))
    late = late[:, :rows].reshape(total, -1)
    out_grad = jnp.einsum(
        "td,tk->dk", late[:, cols:], early[:, :q_cols], preferred_element_type=f32
    )
    qkv_weight_grad = jnp.einsum(
        "td,tk->dk", early[:, q_cols:], late[:, :cols], preferred_element_type=f32
    )
    return (
        mixed,
        tokens_grad,
        attn_gain_grad,
        qkv_weight_grad[:, :q_cols],
        qkv_weight_grad[:, q_cols : q_cols + k_cols],
        qkv_weight_grad[:, q_cols + k_cols :],
        out_grad,
        ffn_gain_grad,
        gate_grad,
        up_grad,
        down_grad,
    )


def solution(mesh):
    placed = (
        P("ep", None),
        P("ep", None),
        P("ep", None),
        P("ep", None),
        P("ep"),
        P("ep", "tp"),
        P("ep", "tp"),
        P("ep", "tp"),
        P("ep", "tp"),
        P("ep"),
        P("ep", None, "tp"),
        P("ep", None, "tp"),
        P("ep", "tp", None),
        P("ep", None),
    )
    return jax.shard_map(
        body,
        mesh=mesh,
        in_specs=placed,
        out_specs=(
            P("ep", None),
            P("ep", None),
            P("ep"),
            P("ep", "tp"),
            P("ep", "tp"),
            P("ep", "tp"),
            P("ep", "tp"),
            P("ep"),
            P("ep", None, "tp"),
            P("ep", None, "tp"),
            P("ep", "tp", None),
        ),
        check_vma=False,
    )
```

```python
import jax
import jax.numpy as jnp
from jax import lax
from jax.sharding import PartitionSpec as P

HEAD_SIZE = 64
NORM_EPSILON = 1e-06
ROPE_BASE = 10000.0
MASKED = -1e30
LANES = 128
SUBLANES = 16
bf16 = jnp.bfloat16
f32 = jnp.float32


def positions_and_mask(segment_row):
    count = segment_row.shape[0]
    index = jnp.arange(count, dtype=jnp.int32)
    same = segment_row[:, None] == segment_row[None, :]
    before = index[None, :] < index[:, None]
    position = jnp.sum((same & before).astype(jnp.int32), axis=1)
    allowed = same & (index[None, :] <= index[:, None])
    return (position, allowed)


def rope_tables(position):
    half = HEAD_SIZE // 2
    steps = jnp.arange(half, dtype=f32) * (2.0 / HEAD_SIZE)
    frequency = jnp.exp(-jnp.log(f32(ROPE_BASE)) * steps)
    angle = position.astype(f32)[:, None] * frequency[None, :]
    return (jnp.cos(angle)[:, None, :], jnp.sin(angle)[:, None, :])


def rotate(values, cosine, sine):
    half = values.shape[-1] // 2
    first = values[..., :half]
    second = values[..., half:]
    return jnp.concatenate(
        [first * cosine - second * sine, second * cosine + first * sine], axis=-1
    )


def rotate_back(values, cosine, sine):
    return rotate(values, cosine, -sine)


def rms_inverse(values):
    return lax.rsqrt(jnp.mean(values * values, axis=-1, keepdims=True) + NORM_EPSILON)


def rms_backward(values, inverse, gain, upstream):
    gain_term = jnp.sum(upstream * values * inverse, axis=0)
    inner = jnp.mean(values * gain * upstream, axis=-1, keepdims=True)
    input_term = inverse * (gain * upstream) - values * inverse * inverse * inverse * inner
    return (input_term, gain_term)


def exchange(blocks, axis):
    return lax.all_to_all(blocks, axis, split_axis=0, concat_axis=0, tiled=True)


def gather_blocks(value, axis):
    count = lax.axis_size(axis)
    return exchange(jnp.broadcast_to(value[None], (count,) + value.shape), axis)


def flip(value, axis, bit):
    count = lax.axis_size(axis)
    return lax.ppermute(value, axis, [(i, i ^ bit) for i in range(count)])


def bits_of(axis):
    count = lax.axis_size(axis)
    return [1 << i for i in range(count.bit_length() - 1)]


def gather_relative(value, axis):
    for bit in reversed(bits_of(axis)):
        value = jnp.stack([value, flip(value, axis, bit)])
    return value


def reduce_relative(value, axis):
    for bit in bits_of(axis):
        value = value[0] + flip(value[1].astype(bf16), axis, bit).astype(f32)
    return value


def reduce_own(value):
    c_at = lax.axis_index("c")
    y_at = lax.axis_index("y")
    n_y = lax.axis_size("y")

    def step(value, at, axis, bit):
        kept = lax.dynamic_index_in_dim(value, at, 0, False)
        sent = lax.dynamic_index_in_dim(value.astype(bf16), 1 - at, 0, False)
        return kept + flip(sent, axis, bit).astype(f32)

    rows, width = value.shape
    value = value.reshape(n_y, 2, rows // (2 * n_y), width).swapaxes(0, 1)
    value = step(value, c_at, "c", 1)
    for bit in reversed(bits_of("y")):
        value = value.reshape((2, bit) + value.shape[-2:])
        value = step(value, (y_at // bit) % 2, "y", bit)
    return value.reshape(value.shape[-2:])


def after(value, *others):
    return lax.optimization_barrier((value,) + others)[0]


def split_pair(value):
    high = lax.reduce_precision(value, 8, 7)
    return (high.astype(bf16), (value - high).astype(bf16))


def pad_to(value, axis, size):
    widths = [(0, 0)] * value.ndim
    widths[axis] = (0, size - value.shape[axis])
    return jnp.pad(value, widths)


EP = ("z", "x")
TP = ("y", "c")


def body(
    tokens,
    segment_ids,
    route_ids,
    route_weights,
    attn_gain,
    query_weight,
    key_projection_matrix,
    value_projection_matrix,
    out_weight,
    ffn_gain,
    gate_weight,
    up_weight,
    down_weight,
    cotangent,
):
    n_z = lax.axis_size("z")
    n_ep = lax.axis_size(EP)
    n_tp = lax.axis_size(TP)
    tp_at = lax.axis_index(TP)
    x_at = lax.axis_index("x")
    rows, width = tokens.shape
    sub = rows // n_tp
    piece = width // n_ep
    half = width // 2
    local_experts, _, _ = gate_weight.shape
    experts = local_experts * n_ep
    total = rows * n_ep
    scale = HEAD_SIZE ** (-0.5)
    q_cols = query_weight.shape[1]
    k_cols = key_projection_matrix.shape[1]

    def own_rows(value):
        return lax.dynamic_slice_in_dim(value, tp_at * sub, sub, 0)

    def features(value, at):
        lead = value.shape[:-1]
        value = value.reshape(lead + (n_z, 2, piece))
        axis = len(lead) + 1
        return lax.dynamic_index_in_dim(value, at, axis, False).reshape(lead + (half,))

    def whole_features(own, other):
        lead = own.shape[:-1]
        own = own.reshape(lead + (n_z, 1, piece))
        other = other.reshape(lead + (n_z, 1, piece))
        first = jnp.where(x_at == 0, own, other)
        second = jnp.where(x_at == 0, other, own)
        return jnp.concatenate([first, second], axis=-2).reshape(lead + (width,))

    shard = jnp.concatenate(
        [query_weight, key_projection_matrix, value_projection_matrix, out_weight], 1
    )
    cols = q_cols + 2 * k_cols
    out_cols = out_weight.shape[1]
    gain_rows = jnp.pad(
        jnp.stack([attn_gain, ffn_gain]), ((0, SUBLANES - 2), (cols, out_cols - piece))
    )
    packed = gather_blocks(jnp.concatenate([shard, gain_rows], 0), "z")
    other_tokens = flip(tokens, "x", 1)
    qkv_half = packed[:, :piece, :cols].reshape(half, cols)
    gain_half = packed[:, piece, cols : cols + piece].reshape(half).astype(f32)
    pair_tokens = jnp.concatenate([tokens, other_tokens], 0).astype(f32)
    pair_inverse = rms_inverse(pair_tokens)
    pair_normed = (features(pair_tokens, x_at) * pair_inverse * gain_half).astype(bf16)
    qkv_part = jnp.dot(pair_normed, qkv_half, preferred_element_type=f32)
    qkv = qkv_part[:rows] + flip(qkv_part[rows:].astype(bf16), "x", 1).astype(f32)

    out_own = packed[:, :, cols:]
    out_other = flip(out_own, "x", 1)
    out_packed = jnp.where(
        x_at == 0, jnp.stack([out_own, out_other], 1), jnp.stack([out_other, out_own], 1)
    )
    out_full = out_packed[:, :, :piece].reshape(width, out_cols)
    gain_one = out_packed[:, :, piece, :piece].reshape(width).astype(f32)
    gain_two = out_packed[:, :, piece + 1, :piece].reshape(width).astype(f32)

    expert_index = jnp.arange(experts, dtype=jnp.int32)
    own_ids = own_rows(route_ids)
    own_weights = own_rows(route_weights)
    dense = jnp.sum(
        jnp.where(own_ids[:, :, None] == expert_index, own_weights[:, :, None], 0.0), axis=1
    )
    dense = dense.reshape(sub, n_ep, local_experts).swapaxes(0, 1)
    dense_high, dense_low = split_pair(dense)
    dense_pack = pad_to(jnp.concatenate([dense_high, dense_low], -1), 2, LANES)
    cot_own = own_rows(cotangent)
    cot_pack = jnp.concatenate(
        [jnp.broadcast_to(cot_own[None], (n_ep, sub, width)), dense_pack], axis=-1
    )
    cot_ep = exchange(after(cot_pack, packed), EP)

    position, allowed = positions_and_mask(segment_ids[0])
    cosine, sine = rope_tables(position)
    query = qkv[:, :q_cols].reshape(rows, -1, HEAD_SIZE)
    keys = qkv[:, q_cols : q_cols + k_cols].reshape(rows, -1, HEAD_SIZE)
    query_rot = rotate(query, cosine, sine).astype(bf16)
    key_rot = rotate(keys, cosine, sine).astype(bf16)
    value_rows = qkv[:, q_cols + k_cols :].astype(bf16).reshape(rows, -1, HEAD_SIZE)
    grouped = query_rot.reshape(rows, key_rot.shape[1], -1, HEAD_SIZE)
    scores = jnp.einsum("thgd,uhd->hgtu", grouped, key_rot, preferred_element_type=f32) * scale
    scores = jnp.where(allowed, scores, MASKED)
    peak = jnp.max(scores, axis=-1, keepdims=True)
    logsum = peak + jnp.log(jnp.sum(jnp.exp(scores - peak), axis=-1, keepdims=True))
    probs = jnp.exp(scores - logsum)
    probs_low = probs.astype(bf16)
    attended = jnp.einsum(
        "hgtu,uhd->thgd", probs_low, value_rows, preferred_element_type=f32
    ).astype(bf16)
    attended_flat = attended.reshape(rows, -1)
    branch_part = jnp.einsum("tk,dk->td", attended_flat, out_full, preferred_element_type=f32)
    branch = reduce_own(branch_part)
    tokens_own = own_rows(tokens).astype(f32)
    hidden_one = tokens_own + branch
    inverse_two = rms_inverse(hidden_one)
    normed_two = (hidden_one * inverse_two * gain_two).astype(bf16)

    rows_ep = gather_blocks(normed_two, EP)
    cot_all = gather_relative(gather_relative(after(cot_ep, normed_two), "y"), "c")
    rows_in = gather_relative(gather_relative(rows_ep, "y"), "c").reshape(total, width)
    cot_all = cot_all.reshape(total, -1)
    weights_all = cot_all[:, width : width + local_experts].astype(f32) + cot_all[
        :, width + local_experts : width + 2 * local_experts
    ].astype(f32)
    cot_all = cot_all[:, :width]
    gate_pre = jnp.einsum("td,edf->tef", rows_in, gate_weight, preferred_element_type=f32)
    up_pre = jnp.einsum("td,edf->tef", rows_in, up_weight, preferred_element_type=f32)
    sigma = jax.nn.sigmoid(gate_pre)
    active = gate_pre * sigma
    route = weights_all[:, :, None]
    hidden = (active * up_pre * route).astype(bf16)
    grad_hidden = (
        jnp.einsum("td,efd->tef", cot_all, down_weight, preferred_element_type=f32) * route
    )
    grad_gate = (grad_hidden * up_pre * sigma * (1.0 + gate_pre * (1.0 - sigma))).astype(bf16)
    grad_up = (grad_hidden * active).astype(bf16)
    grad_in = jnp.einsum("tef,edf->td", grad_gate, gate_weight, preferred_element_type=f32)
    grad_in = grad_in + jnp.einsum("tef,edf->td", grad_up, up_weight, preferred_element_type=f32)
    blocks = (2,) * (n_tp.bit_length() - 1) + (n_ep, sub, width)
    grad_c = reduce_relative(grad_in.reshape(blocks), "c")
    grad_y = reduce_relative(grad_c, "y")
    grad_ep = exchange(grad_y.astype(bf16), EP)

    moe = jnp.einsum("tef,efd->td", hidden, down_weight, preferred_element_type=f32)
    moe_c = reduce_relative(after(moe, grad_c).reshape(blocks), "c")
    moe_y = reduce_relative(after(moe_c, grad_y), "y")
    down_grad = jnp.einsum("tef,td->efd", hidden, cot_all, preferred_element_type=f32)
    gate_grad = jnp.einsum("td,tef->edf", rows_in, grad_gate, preferred_element_type=f32)
    up_grad = jnp.einsum("td,tef->edf", rows_in, grad_up, preferred_element_type=f32)
    grad_ep, down_grad, gate_grad, up_grad, moe_y = lax.optimization_barrier(
        (grad_ep, down_grad, gate_grad, up_grad, moe_y)
    )
    grad_normed_two = jnp.sum(grad_ep.astype(f32), axis=0)

    norm_term, ffn_gain_part = rms_backward(hidden_one, inverse_two, gain_two, grad_normed_two)
    grad_hidden_one = cot_own.astype(f32) + norm_term
    ffn_rows = pad_to(jnp.stack(split_pair(ffn_gain_part)), 0, SUBLANES)
    branch_rows = lax.all_gather(
        jnp.concatenate([grad_hidden_one.astype(bf16), ffn_rows], 0), TP, axis=0
    )
    grad_branch = branch_rows[:, :sub].reshape(rows, width)
    ffn_gain_part = jnp.sum(branch_rows[:, sub : sub + 2].astype(f32), axis=(0, 1))

    attended_other = flip(after(attended_flat, normed_two), "x", 1)
    ffn_pair = pad_to(jnp.stack(split_pair(ffn_gain_part)), 0, SUBLANES)
    branch_pack = jnp.concatenate([grad_branch, ffn_pair], 0)
    branch_other = flip(features(branch_pack, 1 - x_at), "x", 1)
    branch_half = features(branch_pack, x_at)
    out_part = jnp.einsum(
        "td,tk->dk",
        jnp.concatenate([branch_half[:rows], branch_other[:rows]], 0),
        jnp.concatenate([attended_flat, attended_other], 0),
        preferred_element_type=f32,
    )
    ffn_half = jnp.sum(
        branch_half[rows : rows + 2].astype(f32) + branch_other[rows : rows + 2].astype(f32), axis=0
    )
    ffn_half = jnp.stack(split_pair(ffn_half)).reshape(2, n_z, piece).swapaxes(0, 1)

    grad_attended = (
        jnp.dot(grad_branch, out_full, preferred_element_type=f32)
        .astype(bf16)
        .reshape(attended.shape)
    )
    value_grad = jnp.einsum("hgtu,thgd->uhd", probs_low, grad_attended, preferred_element_type=f32)
    grad_probs = jnp.einsum("thgd,uhd->hgtu", grad_attended, value_rows, preferred_element_type=f32)
    delta = jnp.einsum("thgd,thgd->hgt", grad_attended, attended, preferred_element_type=f32)
    grad_scores = (probs * (grad_probs - delta[..., None]) * scale).astype(bf16)
    query_grad_rot = jnp.einsum("hgtu,uhd->thgd", grad_scores, key_rot, preferred_element_type=f32)
    key_grad_rot = jnp.einsum("hgtu,thgd->uhd", grad_scores, grouped, preferred_element_type=f32)
    query_back = rotate_back(query_grad_rot.reshape(rows, -1, HEAD_SIZE), cosine, sine)
    key_back = rotate_back(key_grad_rot, cosine, sine)
    qkv_grad = jnp.concatenate(
        [
            query_back.reshape(rows, -1).astype(bf16),
            key_back.reshape(rows, -1).astype(bf16),
            value_grad.reshape(rows, -1).astype(bf16),
        ],
        axis=1,
    )

    qkv_grad_other = flip(qkv_grad, "x", 1)
    qkv_part = jnp.einsum(
        "td,tk->dk",
        pair_normed,
        jnp.concatenate([qkv_grad, qkv_grad_other], 0),
        preferred_element_type=f32,
    )
    grad_part = jnp.concatenate([qkv_part, out_part], 1).astype(bf16)
    ffn_half = pad_to(pad_to(ffn_half, 2, cols + out_cols), 1, SUBLANES)
    grad_blocks = exchange(
        jnp.concatenate([grad_part.reshape(n_z, piece, cols + out_cols), ffn_half], 1), "z"
    )
    ffn_gain_grad = jnp.sum(grad_blocks[:, piece : piece + 2, :piece].astype(f32), axis=(0, 1))

    def block_sum(start, size):
        return jnp.sum(grad_blocks[:, :piece, start : start + size].astype(f32), axis=0)

    qkv_other_half = flip(after(qkv_half, rows_ep), "x", 1)
    normed_part = whole_features(
        jnp.einsum("tk,dk->td", qkv_grad, qkv_half, preferred_element_type=f32),
        jnp.einsum("tk,dk->td", qkv_grad, qkv_other_half, preferred_element_type=f32),
    )
    grad_normed_one = reduce_own(normed_part)
    input_term = rms_backward(
        tokens_own, own_rows(pair_inverse[:rows]), gain_one, grad_normed_one
    )[0]
    moe_ep = exchange(after(moe_y, grad_ep).astype(bf16), EP)
    moe_own = jnp.sum(moe_ep.astype(f32), axis=0)
    mixed_own = (hidden_one + moe_own).astype(bf16)
    last_rows = lax.all_gather(
        jnp.concatenate([(grad_hidden_one + input_term).astype(bf16), mixed_own], 0),
        TP,
        axis=0,
    )
    tokens_grad = last_rows[:, :sub].reshape(rows, width).astype(f32)
    mixed = last_rows[:, sub : 2 * sub].reshape(rows, width)

    gain_part = jnp.sum(block_sum(0, cols) * shard[:, :cols].astype(f32), axis=1)
    gain_part = (gain_part / attn_gain.astype(f32)).reshape(1, piece)
    attn_gain_grad = jnp.sum(lax.all_gather(gain_part, TP, axis=0), axis=(0, 1))
    return (
        mixed,
        tokens_grad,
        attn_gain_grad,
        block_sum(0, q_cols),
        block_sum(q_cols, k_cols),
        block_sum(q_cols + k_cols, k_cols),
        block_sum(cols, out_cols),
        ffn_gain_grad,
        gate_grad,
        up_grad,
        down_grad,
    )


def solution(mesh):
    n_ep, n_tp = mesh.devices.shape
    split = jax.sharding.Mesh(
        mesh.devices.reshape(n_ep // 2, 2, n_tp // 2, 2), ("z", "x", "y", "c")
    )
    return jax.shard_map(
        body,
        mesh=split,
        in_specs=(
            P(EP, None),
            P(EP, None),
            P(EP, None),
            P(EP, None),
            P(EP),
            P(EP, TP),
            P(EP, TP),
            P(EP, TP),
            P(EP, TP),
            P(EP),
            P(EP, None, TP),
            P(EP, None, TP),
            P(EP, TP, None),
            P(EP, None),
        ),
        out_specs=(
            P(EP, None),
            P(EP, None),
            P(EP),
            P(EP, TP),
            P(EP, TP),
            P(EP, TP),
            P(EP, TP),
            P(EP),
            P(EP, None, TP),
            P(EP, None, TP),
            P(EP, TP, None),
        ),
        check_vma=False,
    )
```

```python
import jax
import jax.numpy as jnp
from jax import lax
from jax.experimental import pallas as pl
from jax.experimental.pallas import tpu as pltpu
from jax.sharding import PartitionSpec as P

HEAD_SIZE = 64
NORM_EPSILON = 1e-06
ROPE_BASE = 10000.0
MASKED = -1e30
LANES = 128
SUBLANES = 16
bf16 = jnp.bfloat16
f32 = jnp.float32


def positions_and_mask(segment_row):
    count = segment_row.shape[0]
    index = jnp.arange(count, dtype=jnp.int32)
    same = segment_row[:, None] == segment_row[None, :]
    before = index[None, :] < index[:, None]
    position = jnp.sum((same & before).astype(jnp.int32), axis=1)
    allowed = same & (index[None, :] <= index[:, None])
    return (position, allowed)


def rope_tables(position):
    half = HEAD_SIZE // 2
    steps = jnp.arange(half, dtype=f32) * (2.0 / HEAD_SIZE)
    frequency = jnp.exp(-jnp.log(f32(ROPE_BASE)) * steps)
    angle = position.astype(f32)[:, None] * frequency[None, :]
    return (jnp.cos(angle)[:, None, :], jnp.sin(angle)[:, None, :])


def rotate(values, cosine, sine):
    half = values.shape[-1] // 2
    first = values[..., :half]
    second = values[..., half:]
    return jnp.concatenate(
        [first * cosine - second * sine, second * cosine + first * sine], axis=-1
    )


def rotate_back(values, cosine, sine):
    return rotate(values, cosine, -sine)


def rms_inverse(values):
    return lax.rsqrt(jnp.mean(values * values, axis=-1, keepdims=True) + NORM_EPSILON)


def rms_backward(values, inverse, gain, upstream):
    gain_term = jnp.sum(upstream * values * inverse, axis=0)
    inner = jnp.mean(values * gain * upstream, axis=-1, keepdims=True)
    input_term = inverse * (gain * upstream) - values * inverse * inverse * inverse * inner
    return (input_term, gain_term)


def exchange(blocks, axis):
    return lax.all_to_all(blocks, axis, split_axis=0, concat_axis=0, tiled=True)


def gather_blocks(value, axis):
    count = lax.axis_size(axis)
    return exchange(jnp.broadcast_to(value[None], (count,) + value.shape), axis)


def flip(value, axis, bit):
    count = lax.axis_size(axis)
    return lax.ppermute(value, axis, [(i, i ^ bit) for i in range(count)])


def bits_of(axis):
    count = lax.axis_size(axis)
    return [1 << i for i in range(count.bit_length() - 1)]


def contract(left, right, left_axis, right_axis):
    return lax.dot_general(
        left, right, (((left_axis,), (right_axis,)), ((), ())), preferred_element_type=f32
    )


def side_by_side(ref):
    return jnp.concatenate([ref[i] for i in range(ref.shape[0])], axis=1)


def expert_kernel(
    x_a, x_b, c_a, c_b, gate, up, down,
    grad_a, grad_b, moe_a, moe_b, hidden, grad_gate, grad_up,
):
    rows, width = x_a.shape
    count, units, _ = down.shape
    gate_all = side_by_side(gate)
    up_all = side_by_side(up)
    down_all = down[...].reshape(count * units, width)
    for i, (x_ref, c_ref) in enumerate(((x_a, c_a), (x_b, c_b))):
        part = pl.ds(i * rows, rows)
        gate_pre = contract(x_ref[...], gate_all, 1, 0)
        up_pre = contract(x_ref[...], up_all, 1, 0)
        grad_hidden = contract(c_ref[:, :width], down_all, 1, 1)
        pack = c_ref[:, width:].astype(f32)
        weights = [
            jnp.broadcast_to(pack[:, e : e + 1] + pack[:, count + e : count + e + 1], (rows, units))
            for e in range(count)
        ]
        weight = jnp.concatenate(weights, axis=1)
        grad_hidden = grad_hidden * weight
        sigma = jax.nn.sigmoid(gate_pre)
        active = gate_pre * sigma
        low = (active * up_pre * weight).astype(bf16)
        low_gate = (grad_hidden * up_pre * sigma * (1.0 + gate_pre * (1.0 - sigma))).astype(bf16)
        low_up = (grad_hidden * active).astype(bf16)
        hidden[part] = low
        grad_gate[part] = low_gate
        grad_up[part] = low_up
        grad = contract(low_gate, gate_all, 1, 1) + contract(low_up, up_all, 1, 1)
        moe = contract(low, down_all, 1, 0)
        if i == 0:
            grad_a[...] = grad
            moe_a[...] = moe.astype(bf16)
        else:
            grad_b[...] = grad.astype(bf16)
            moe_b[...] = moe.astype(bf16)


def run_experts(x_a, x_b, c_a, c_b, gate, up, down):
    rows, width = x_a.shape
    count, _, units = gate.shape
    whole = pl.BlockSpec(memory_space=pltpu.VMEM)
    low = jax.ShapeDtypeStruct((rows, width), bf16)
    held = jax.ShapeDtypeStruct((2 * rows, count * units), bf16)
    return pl.pallas_call(
        expert_kernel,
        in_specs=[whole] * 7,
        out_specs=[whole] * 7,
        out_shape=[jax.ShapeDtypeStruct((rows, width), f32), low, low, low, held, held, held],
    )(x_a, x_b, c_a, c_b, gate, up, down)


def grads_kernel(*refs):
    gate_out, up_out, down_out, turned = refs[-4:]
    groups = (len(refs) - 4) // 7
    x_refs, c_refs = refs[: 2 * groups], refs[2 * groups : 4 * groups]
    hidden, grad_gate, grad_up = (refs[(4 + i) * groups : (5 + i) * groups] for i in range(3))
    rows, width = x_refs[0].shape

    @pl.when(pl.program_id(0) == 0)
    def _():
        for i, ref in enumerate(x_refs):
            turned[:, i * rows : (i + 1) * rows] = ref[...].T

    gate_sum = up_sum = down_sum = 0.0
    for k in range(groups):
        columns = turned[:, 2 * k * rows : 2 * (k + 1) * rows]
        gate_sum = gate_sum + contract(columns, grad_gate[k][...], 1, 0)
        up_sum = up_sum + contract(columns, grad_up[k][...], 1, 0)
        for i in range(2):
            low = hidden[k][i * rows : (i + 1) * rows]
            down_sum = down_sum + contract(low, c_refs[2 * k + i][:, :width], 0, 0)
    gate_out[0] = gate_sum
    up_out[0] = up_sum
    down_out[0] = down_sum


def run_grads(x_parts, c_parts, hidden, grad_gate, grad_up, count):
    rows, width = x_parts[0].shape
    units = hidden[0].shape[1] // count
    whole = pl.BlockSpec(memory_space=pltpu.VMEM)
    tall = pl.BlockSpec((1, width, units), lambda e: (e, 0, 0))
    wide = pl.BlockSpec((1, units, width), lambda e: (e, 0, 0))
    per_expert = pl.BlockSpec((2 * rows, units), lambda e: (0, e))
    parts = len(x_parts)
    return pl.pallas_call(
        grads_kernel,
        grid=(count,),
        in_specs=[whole] * (2 * parts) + [per_expert] * (3 * parts // 2),
        out_specs=[tall, tall, wide],
        out_shape=[
            jax.ShapeDtypeStruct((count, width, units), f32),
            jax.ShapeDtypeStruct((count, width, units), f32),
            jax.ShapeDtypeStruct((count, units, width), f32),
        ],
        scratch_shapes=[pltpu.VMEM((width, parts * rows), bf16)],
    )(*x_parts, *c_parts, *hidden, *grad_gate, *grad_up)


def gather_offsets(value):
    blocks = {0: value}
    for bit in reversed(bits_of("y")):
        blocks.update({k | bit: flip(v, "y", bit) for k, v in blocks.items()})
    return blocks


def reduce_offsets(blocks):
    for bit in bits_of("y"):
        for k in [k for k in blocks if k & bit]:
            sent = flip(blocks.pop(k).astype(bf16), "y", bit)
            blocks[k ^ bit] = blocks[k ^ bit] + sent.astype(f32)
    return blocks[0]


def reduce_axis(value, axis):
    at = lax.axis_index(axis)
    rest = value.shape[1:]
    for bit in reversed(bits_of(axis)):
        side = (at // bit) % 2
        value = value.reshape((2, bit) + rest)
        sent = jnp.where(side == 0, value[1], value[0]).astype(bf16)
        kept = jnp.where(side == 0, value[0], value[1])
        received = flip(sent, axis, bit)
        value = kept + received.astype(f32)
    return value.reshape(rest)


def reduce_own(value):
    rows, width = value.shape
    n_y = lax.axis_size("y")
    value = value.reshape(n_y, 2, rows // (2 * n_y), width).swapaxes(0, 1)
    return reduce_axis(reduce_axis(value, "c"), "y")


def after(value, *others):
    return lax.optimization_barrier((value,) + others)[0]


def split_pair(value):
    high = lax.reduce_precision(value, 8, 7)
    return (high.astype(bf16), (value - high).astype(bf16))


def pad_to(value, axis, size):
    widths = [(0, 0)] * value.ndim
    widths[axis] = (0, size - value.shape[axis])
    return jnp.pad(value, widths)


EP = ("z", "x")
TP = ("y", "c")


def body(
    tokens,
    segment_ids,
    route_ids,
    route_weights,
    attn_gain,
    query_weight,
    key_projection_matrix,
    value_projection_matrix,
    out_weight,
    ffn_gain,
    gate_weight,
    up_weight,
    down_weight,
    cotangent,
):
    n_z = lax.axis_size("z")
    n_ep = lax.axis_size(EP)
    n_tp = lax.axis_size(TP)
    tp_at = lax.axis_index(TP)
    x_at = lax.axis_index("x")
    rows, width = tokens.shape
    sub = rows // n_tp
    piece = width // n_ep
    half = width // 2
    local_experts, _, _ = gate_weight.shape
    experts = local_experts * n_ep
    scale = HEAD_SIZE ** (-0.5)
    q_cols = query_weight.shape[1]
    k_cols = key_projection_matrix.shape[1]

    def own_rows(value):
        return lax.dynamic_slice_in_dim(value, tp_at * sub, sub, 0)

    def features(value, at):
        pieces = []
        for z in range(n_z):
            first = value[..., 2 * z * piece : (2 * z + 1) * piece]
            second = value[..., (2 * z + 1) * piece : (2 * z + 2) * piece]
            pieces.append(jnp.where(at == 0, first, second))
        return jnp.concatenate(pieces, axis=-1)

    def whole_features(own, other):
        pieces = []
        for z in range(n_z):
            mine = own[..., z * piece : (z + 1) * piece]
            theirs = other[..., z * piece : (z + 1) * piece]
            pieces += [jnp.where(x_at == 0, mine, theirs), jnp.where(x_at == 0, theirs, mine)]
        return jnp.concatenate(pieces, axis=-1)

    shard = jnp.concatenate(
        [query_weight, key_projection_matrix, value_projection_matrix, out_weight], 1
    )
    cols = q_cols + 2 * k_cols
    out_cols = out_weight.shape[1]
    gain_rows = jnp.pad(
        jnp.stack([attn_gain, ffn_gain]), ((0, SUBLANES - 2), (cols, out_cols - piece))
    )
    packed = gather_blocks(jnp.concatenate([shard, gain_rows], 0), "z")
    other_tokens = flip(tokens, "x", 1)
    qkv_half = packed[:, :piece, :cols].reshape(half, cols)
    gain_half = packed[:, piece, cols : cols + piece].reshape(half).astype(f32)
    pair_tokens = jnp.concatenate([tokens, other_tokens], 0).astype(f32)
    pair_inverse = rms_inverse(pair_tokens)
    pair_normed = (features(pair_tokens, x_at) * pair_inverse * gain_half).astype(bf16)
    qkv_part = jnp.dot(pair_normed, qkv_half, preferred_element_type=f32)
    qkv = qkv_part[:rows] + flip(qkv_part[rows:].astype(bf16), "x", 1).astype(f32)

    out_own = packed[:, :, cols:]
    out_other = flip(out_own, "x", 1)
    out_packed = jnp.where(
        x_at == 0, jnp.stack([out_own, out_other], 1), jnp.stack([out_other, out_own], 1)
    )
    out_full = out_packed[:, :, :piece].reshape(width, out_cols)
    gain_one = out_packed[:, :, piece, :piece].reshape(width).astype(f32)
    gain_two = out_packed[:, :, piece + 1, :piece].reshape(width).astype(f32)

    expert_index = jnp.arange(experts, dtype=jnp.int32)
    own_ids = own_rows(route_ids)
    own_weights = own_rows(route_weights)
    dense = jnp.sum(
        jnp.where(own_ids[:, :, None] == expert_index, own_weights[:, :, None], 0.0), axis=1
    )
    dense = dense.reshape(sub, n_ep, local_experts).swapaxes(0, 1)
    dense_high, dense_low = split_pair(dense)
    dense_pack = jnp.concatenate([dense_high, dense_low], -1)
    dense_pack = dense_pack.reshape(n_z, 2, sub, 2 * local_experts)
    dense_pack = pad_to(jnp.concatenate([dense_pack[:, 0], dense_pack[:, 1]], -1), 2, LANES)
    cot_own = own_rows(cotangent)
    cot_pack = jnp.concatenate(
        [jnp.broadcast_to(cot_own[None], (n_z, sub, width)), dense_pack], axis=-1
    )
    cot_z = exchange(after(cot_pack, packed), "z")
    cot_x = flip(cot_z, "x", 1)
    cot_ep = jnp.where(x_at == 0, jnp.stack([cot_z, cot_x], 1), jnp.stack([cot_x, cot_z], 1))
    routed = cot_ep[..., width:]
    routed = jnp.where(
        x_at == 0, routed[..., : 2 * local_experts], routed[..., 2 * local_experts : 4 * local_experts]
    )
    cot_ep = jnp.concatenate([cot_ep[..., :width], pad_to(routed, 3, LANES)], axis=-1)
    cot_ep = cot_ep.reshape(n_ep * sub, width + LANES)

    position, allowed = positions_and_mask(segment_ids[0])
    cosine, sine = rope_tables(position)
    query = qkv[:, :q_cols].reshape(rows, -1, HEAD_SIZE)
    keys = qkv[:, q_cols : q_cols + k_cols].reshape(rows, -1, HEAD_SIZE)
    query_rot = rotate(query, cosine, sine).astype(bf16)
    key_rot = rotate(keys, cosine, sine).astype(bf16)
    value_rows = qkv[:, q_cols + k_cols :].astype(bf16).reshape(rows, -1, HEAD_SIZE)
    grouped = query_rot.reshape(rows, key_rot.shape[1], -1, HEAD_SIZE)
    scores = jnp.einsum("thgd,uhd->hgtu", grouped, key_rot, preferred_element_type=f32) * scale
    scores = jnp.where(allowed, scores, MASKED)
    peak = jnp.max(scores, axis=-1, keepdims=True)
    logsum = peak + jnp.log(jnp.sum(jnp.exp(scores - peak), axis=-1, keepdims=True))
    probs = jnp.exp(scores - logsum)
    probs_low = probs.astype(bf16)
    attended = jnp.einsum(
        "hgtu,uhd->thgd", probs_low, value_rows, preferred_element_type=f32
    ).astype(bf16)
    attended_flat = attended.reshape(rows, -1)
    branch_part = jnp.einsum("tk,dk->td", attended_flat, out_full, preferred_element_type=f32)
    branch = reduce_own(branch_part)
    tokens_own = own_rows(tokens).astype(f32)
    hidden_one = tokens_own + branch
    inverse_two = rms_inverse(hidden_one)
    normed_two = (hidden_one * inverse_two * gain_two).astype(bf16)

    rows_ep = gather_blocks(normed_two, EP).reshape(n_ep * sub, width)
    cot_parts = gather_offsets(cot_ep)
    row_parts = gather_offsets(rows_ep)
    offsets = sorted(row_parts)
    results = {}
    for k in offsets:
        cot_other = flip(cot_parts[k], "c", 1)
        row_other = flip(row_parts[k], "c", 1)
        parts = (row_parts[k], row_other, cot_parts[k], cot_other)
        results[k] = parts + tuple(run_experts(*parts, gate_weight, up_weight, down_weight))
    grad_c = {k: r[4] + flip(r[5], "c", 1).astype(f32) for k, r in results.items()}
    grad_c[0] = lax.optimization_barrier(grad_c[0])
    grad_y = reduce_offsets(dict(grad_c)).astype(bf16)
    moe_c = {k: r[6].astype(f32) + flip(r[7], "c", 1).astype(f32) for k, r in results.items()}
    moe_y = reduce_offsets(moe_c).astype(bf16).reshape(n_ep, sub, width)
    ordered_results = [results[k] for k in offsets]
    gate_grad, up_grad, down_grad = run_grads(
        [part for r in ordered_results for part in r[:2]],
        [part for r in ordered_results for part in r[2:4]],
        *([r[i] for r in ordered_results] for i in (8, 9, 10)),
        local_experts,
    )
    grad_y, gate_grad, up_grad, down_grad = lax.optimization_barrier(
        (grad_y, gate_grad, up_grad, down_grad)
    )
    grad_ep = exchange(grad_y.reshape(n_ep, sub, width), EP)
    grad_normed_two = jnp.sum(grad_ep.astype(f32), axis=0)

    norm_term, ffn_gain_part = rms_backward(hidden_one, inverse_two, gain_two, grad_normed_two)
    grad_hidden_one = cot_own.astype(f32) + norm_term
    ffn_rows = pad_to(jnp.stack(split_pair(ffn_gain_part)), 0, SUBLANES)
    branch_rows = lax.all_gather(
        jnp.concatenate([grad_hidden_one.astype(bf16), ffn_rows], 0), TP, axis=0
    )
    grad_branch = branch_rows[:, :sub].reshape(rows, width)
    ffn_gain_part = jnp.sum(branch_rows[:, sub : sub + 2].astype(f32), axis=(0, 1))

    attended_other = flip(after(attended_flat, normed_two), "x", 1)
    branch_other = flip(features(grad_branch, 1 - x_at), "x", 1)
    branch_half = features(grad_branch, x_at)
    out_part = jnp.einsum(
        "td,tk->dk",
        jnp.concatenate([branch_half, branch_other], 0),
        jnp.concatenate([attended_flat, attended_other], 0),
        preferred_element_type=f32,
    )

    grad_attended = jnp.dot(grad_branch, out_full, preferred_element_type=f32)
    grad_attended = grad_attended.astype(bf16).reshape(attended.shape)
    value_grad = jnp.einsum("hgtu,thgd->uhd", probs_low, grad_attended, preferred_element_type=f32)
    grad_probs = jnp.einsum("thgd,uhd->hgtu", grad_attended, value_rows, preferred_element_type=f32)
    delta = jnp.einsum("thgd,thgd->hgt", grad_attended, attended, preferred_element_type=f32)
    grad_scores = (probs * (grad_probs - delta[..., None]) * scale).astype(bf16)
    query_grad_rot = jnp.einsum("hgtu,uhd->thgd", grad_scores, key_rot, preferred_element_type=f32)
    key_grad_rot = jnp.einsum("hgtu,thgd->uhd", grad_scores, grouped, preferred_element_type=f32)
    query_back = rotate_back(query_grad_rot.reshape(rows, -1, HEAD_SIZE), cosine, sine)
    key_back = rotate_back(key_grad_rot, cosine, sine)
    qkv_grad = jnp.concatenate(
        [
            query_back.reshape(rows, -1).astype(bf16),
            key_back.reshape(rows, -1).astype(bf16),
            value_grad.reshape(rows, -1).astype(bf16),
        ],
        axis=1,
    )

    qkv_grad_other = flip(qkv_grad, "x", 1)
    qkv_part = jnp.einsum(
        "td,tk->dk",
        pair_normed,
        jnp.concatenate([qkv_grad, qkv_grad_other], 0),
        preferred_element_type=f32,
    )
    grad_part = jnp.concatenate([qkv_part, out_part], 1).astype(bf16)
    grad_blocks = exchange(grad_part.reshape(n_z, piece, cols + out_cols), "z")

    def block_sum(start, size):
        return jnp.sum(grad_blocks[:, :, start : start + size].astype(f32), axis=0)

    qkv_other_half = flip(after(qkv_half, rows_ep), "x", 1)
    normed_part = whole_features(
        jnp.einsum("tk,dk->td", qkv_grad, qkv_half, preferred_element_type=f32),
        jnp.einsum("tk,dk->td", qkv_grad, qkv_other_half, preferred_element_type=f32),
    )
    grad_normed_one = reduce_own(normed_part)
    input_term, attn_gain_part = rms_backward(
        tokens_own, own_rows(pair_inverse[:rows]), gain_one, grad_normed_one
    )
    attn_rows = pad_to(jnp.stack(split_pair(attn_gain_part)), 0, SUBLANES)
    moe_ep = exchange(after(moe_y, grad_ep), EP)
    moe_own = jnp.sum(moe_ep.astype(f32), axis=0)
    mixed_own = (hidden_one + moe_own).astype(bf16)
    last_rows = lax.all_gather(
        jnp.concatenate(
            [(grad_hidden_one + input_term).astype(bf16), mixed_own, attn_rows], 0
        ),
        TP,
        axis=0,
    )
    tokens_grad = last_rows[:, :sub].reshape(rows, width).astype(f32)
    mixed = last_rows[:, sub : 2 * sub].reshape(rows, width)
    gain_sum = jnp.sum(last_rows[:, 2 * sub : 2 * sub + 2].astype(f32), axis=(0, 1))
    gain_sum = jnp.stack([gain_sum, ffn_gain_part]).reshape(2, -1, LANES)
    gain_sum = gain_sum + flip(gain_sum, "x", 1)
    for bit in bits_of("z"):
        gain_sum = gain_sum + flip(gain_sum, "z", bit)
    both_gains = lax.dynamic_slice_in_dim(
        gain_sum.reshape(2, width), lax.axis_index(EP) * piece, piece, 1
    )
    attn_gain_grad, ffn_gain_grad = both_gains[0], both_gains[1]
    return (
        mixed,
        tokens_grad,
        attn_gain_grad,
        block_sum(0, q_cols),
        block_sum(q_cols, k_cols),
        block_sum(q_cols + k_cols, k_cols),
        block_sum(cols, out_cols),
        ffn_gain_grad,
        gate_grad,
        up_grad,
        down_grad,
    )


def solution(mesh):
    n_ep, n_tp = mesh.devices.shape
    split = jax.sharding.Mesh(
        mesh.devices.reshape(n_ep // 2, 2, n_tp // 2, 2), ("z", "x", "y", "c")
    )
    return jax.shard_map(
        body,
        mesh=split,
        in_specs=(
            P(EP, None),
            P(EP, None),
            P(EP, None),
            P(EP, None),
            P(EP),
            P(EP, TP),
            P(EP, TP),
            P(EP, TP),
            P(EP, TP),
            P(EP),
            P(EP, None, TP),
            P(EP, None, TP),
            P(EP, TP, None),
            P(EP, None),
        ),
        out_specs=(
            P(EP, None),
            P(EP, None),
            P(EP),
            P(EP, TP),
            P(EP, TP),
            P(EP, TP),
            P(EP, TP),
            P(EP),
            P(EP, None, TP),
            P(EP, None, TP),
            P(EP, TP, None),
        ),
        check_vma=False,
    )
```

```python
import jax
import jax.numpy as jnp
from jax import lax
from jax.experimental import pallas as pl
from jax.experimental.pallas import tpu as pltpu
from jax.sharding import PartitionSpec as P

HEAD_SIZE = 64
NORM_EPSILON = 1e-06
ROPE_BASE = 10000.0
MASKED = -1e30
LANES = 128
SUBLANES = 8
bf16 = jnp.bfloat16
f32 = jnp.float32


def positions_and_mask(segment_row):
    count = segment_row.shape[0]
    index = jnp.arange(count, dtype=jnp.int32)
    same = segment_row[:, None] == segment_row[None, :]
    before = index[None, :] < index[:, None]
    position = jnp.sum((same & before).astype(jnp.int32), axis=1)
    allowed = same & (index[None, :] <= index[:, None])
    return (position, allowed)


def rope_tables(position):
    half = HEAD_SIZE // 2
    steps = jnp.arange(half, dtype=f32) * (2.0 / HEAD_SIZE)
    frequency = jnp.exp(-jnp.log(f32(ROPE_BASE)) * steps)
    angle = position.astype(f32)[:, None] * frequency[None, :]
    return (jnp.cos(angle)[:, None, :], jnp.sin(angle)[:, None, :])


def rotate(values, cosine, sine):
    half = values.shape[-1] // 2
    first = values[..., :half]
    second = values[..., half:]
    return jnp.concatenate(
        [first * cosine - second * sine, second * cosine + first * sine], axis=-1
    )


def rotate_back(values, cosine, sine):
    return rotate(values, cosine, -sine)


def rms_inverse(values):
    return lax.rsqrt(jnp.mean(values * values, axis=-1, keepdims=True) + NORM_EPSILON)


def rms_backward(values, inverse, gain, upstream):
    gain_term = jnp.sum(upstream * values * inverse, axis=0)
    inner = jnp.mean(values * gain * upstream, axis=-1, keepdims=True)
    input_term = inverse * (gain * upstream) - values * inverse * inverse * inverse * inner
    return (input_term, gain_term)


def exchange(blocks, axis):
    return lax.all_to_all(blocks, axis, split_axis=0, concat_axis=0, tiled=True)


def gather_blocks(value, axis):
    count = lax.axis_size(axis)
    return exchange(jnp.broadcast_to(value[None], (count,) + value.shape), axis)


def flip(value, axis, bit):
    count = lax.axis_size(axis)
    return lax.ppermute(value, axis, [(i, i ^ bit) for i in range(count)])


def bits_of(axis):
    count = lax.axis_size(axis)
    return [1 << i for i in range(count.bit_length() - 1)]


def contract(left, right, left_axis, right_axis):
    return lax.dot_general(
        left, right, (((left_axis,), (right_axis,)), ((), ())), preferred_element_type=f32
    )


def side_by_side(ref):
    return jnp.concatenate([ref[i] for i in range(ref.shape[0])], axis=1)


def expert_kernel(
    x_a, x_b, c_a, c_b, gate, up, down,
    grad_a, grad_b, hidden, grad_gate, grad_up,
):
    rows, width = x_a.shape
    count, units, _ = down.shape
    gate_all = side_by_side(gate)
    up_all = side_by_side(up)
    down_all = down[...].reshape(count * units, width)
    for i, (x_ref, c_ref) in enumerate(((x_a, c_a), (x_b, c_b))):
        part = pl.ds(i * rows, rows)
        gate_pre = contract(x_ref[...], gate_all, 1, 0)
        up_pre = contract(x_ref[...], up_all, 1, 0)
        grad_hidden = contract(c_ref[:, :width], down_all, 1, 1)
        pack = c_ref[:, width:].astype(f32)
        weights = [
            jnp.broadcast_to(pack[:, e : e + 1] + pack[:, count + e : count + e + 1], (rows, units))
            for e in range(count)
        ]
        weight = jnp.concatenate(weights, axis=1)
        grad_hidden = grad_hidden * weight
        sigma = jax.nn.sigmoid(gate_pre)
        active = gate_pre * sigma
        low = (active * up_pre * weight).astype(bf16)
        low_gate = (grad_hidden * up_pre * sigma * (1.0 + gate_pre * (1.0 - sigma))).astype(bf16)
        low_up = (grad_hidden * active).astype(bf16)
        hidden[part] = low
        grad_gate[part] = low_gate
        grad_up[part] = low_up
        grad = contract(low_gate, gate_all, 1, 1) + contract(low_up, up_all, 1, 1)
        if i == 0:
            grad_a[...] = grad
        else:
            grad_b[...] = grad.astype(bf16)


def run_experts(x_a, x_b, c_a, c_b, gate, up, down):
    rows, width = x_a.shape
    count, _, units = gate.shape
    whole = pl.BlockSpec(memory_space=pltpu.VMEM)
    low = pltpu.VMEM((rows, width), bf16)
    held = jax.ShapeDtypeStruct((2 * rows, count * units), bf16)
    return pl.pallas_call(
        expert_kernel,
        in_specs=[whole] * 7,
        out_specs=[whole] * 5,
        out_shape=[pltpu.VMEM((rows, width), f32), low, held, held, held],
    )(x_a, x_b, c_a, c_b, gate, up, down)


def grads_kernel(*refs):
    gate_out, up_out, down_out, turned = refs[-4:]
    groups = (len(refs) - 4) // 7
    x_refs, c_refs = refs[: 2 * groups], refs[2 * groups : 4 * groups]
    hidden, grad_gate, grad_up = (refs[(4 + i) * groups : (5 + i) * groups] for i in range(3))
    rows, width = x_refs[0].shape

    @pl.when(pl.program_id(0) == 0)
    def _():
        for i, ref in enumerate(x_refs):
            turned[:, i * rows : (i + 1) * rows] = ref[...].T

    gate_sum = up_sum = down_sum = 0.0
    for k in range(groups):
        columns = turned[:, 2 * k * rows : 2 * (k + 1) * rows]
        gate_sum = gate_sum + contract(columns, grad_gate[k][...], 1, 0)
        up_sum = up_sum + contract(columns, grad_up[k][...], 1, 0)
        for i in range(2):
            low = hidden[k][i * rows : (i + 1) * rows]
            down_sum = down_sum + contract(low, c_refs[2 * k + i][:, :width], 0, 0)
    gate_out[0] = gate_sum
    up_out[0] = up_sum
    down_out[0] = down_sum


def run_grads(x_parts, c_parts, hidden, grad_gate, grad_up, count):
    rows, width = x_parts[0].shape
    units = hidden[0].shape[1] // count
    whole = pl.BlockSpec(memory_space=pltpu.VMEM)
    tall = pl.BlockSpec((1, width, units), lambda e: (e, 0, 0))
    wide = pl.BlockSpec((1, units, width), lambda e: (e, 0, 0))
    per_expert = pl.BlockSpec((2 * rows, units), lambda e: (0, e))
    parts = len(x_parts)
    return pl.pallas_call(
        grads_kernel,
        grid=(count,),
        in_specs=[whole] * (2 * parts) + [per_expert] * (3 * parts // 2),
        out_specs=[tall, tall, wide],
        out_shape=[
            jax.ShapeDtypeStruct((count, width, units), f32),
            jax.ShapeDtypeStruct((count, width, units), f32),
            jax.ShapeDtypeStruct((count, units, width), f32),
        ],
        scratch_shapes=[pltpu.VMEM((width, parts * rows), bf16)],
    )(*x_parts, *c_parts, *hidden, *grad_gate, *grad_up)


def pack_kernel(query, keys, values, out, attn_gain, ffn_gain, packed):
    copies = packed.shape[0]
    piece = query.shape[0]
    spare = packed.shape[1] - piece
    row = lax.broadcasted_iota(jnp.int32, (spare, piece), 0)
    first = jnp.broadcast_to(attn_gain[...].astype(f32), (spare, piece))
    second = jnp.broadcast_to(ffn_gain[...].astype(f32), (spare, piece))
    gains = jnp.where(row == 0, first, jnp.where(row == 1, second, 0.0)).astype(bf16)
    for i in range(copies):
        start = 0
        for ref in (query, keys, values, out):
            packed[i, :piece, start : start + ref.shape[1]] = ref[...]
            start += ref.shape[1]
        start -= out.shape[1]
        packed[i, piece:] = jnp.zeros((spare, packed.shape[2]), bf16)
        packed[i, piece:, start : start + piece] = gains


def pack_weights(copies, query, keys, values, out, attn_gain, ffn_gain):
    piece = query.shape[0]
    width = query.shape[1] + keys.shape[1] + values.shape[1] + out.shape[1]
    return pl.pallas_call(
        pack_kernel,
        out_shape=jax.ShapeDtypeStruct((copies, piece + SUBLANES, width), bf16),
    )(query, keys, values, out, attn_gain[None], ffn_gain[None])


def gather_offsets(value):
    blocks = {0: value}
    for bit in reversed(bits_of("y")):
        blocks.update({k | bit: flip(v, "y", bit) for k, v in blocks.items()})
    return blocks


def reduce_offsets(blocks):
    for bit in bits_of("y"):
        for k in [k for k in blocks if k & bit]:
            sent = flip(blocks.pop(k).astype(bf16), "y", bit)
            blocks[k ^ bit] = blocks[k ^ bit] + sent.astype(f32)
    return blocks[0]


def reduce_axis(value, axis):
    at = lax.axis_index(axis)
    rest = value.shape[1:]
    for bit in reversed(bits_of(axis)):
        side = (at // bit) % 2
        value = value.reshape((2, bit) + rest)
        sent = jnp.where(side == 0, value[1], value[0]).astype(bf16)
        kept = jnp.where(side == 0, value[0], value[1])
        received = flip(sent, axis, bit)
        value = kept + received.astype(f32)
    return value.reshape(rest)


def reduce_own(value):
    rows, width = value.shape
    n_y = lax.axis_size("y")
    value = value.reshape(n_y, 2, rows // (2 * n_y), width).swapaxes(0, 1)
    return reduce_axis(reduce_axis(value, "c"), "y")


def after(value, *others):
    return lax.optimization_barrier((value,) + others)[0]


def split_pair(value):
    high = lax.reduce_precision(value, 8, 7)
    return (high.astype(bf16), (value - high).astype(bf16))


def pad_to(value, axis, size):
    widths = [(0, 0)] * value.ndim
    widths[axis] = (0, size - value.shape[axis])
    return jnp.pad(value, widths)


EP = ("z", "x")
TP = ("y", "c")


def body(
    tokens,
    segment_ids,
    route_ids,
    route_weights,
    attn_gain,
    query_weight,
    key_projection_matrix,
    value_projection_matrix,
    out_weight,
    ffn_gain,
    gate_weight,
    up_weight,
    down_weight,
    cotangent,
):
    n_z = lax.axis_size("z")
    n_ep = lax.axis_size(EP)
    n_tp = lax.axis_size(TP)
    tp_at = lax.axis_index(TP)
    x_at = lax.axis_index("x")
    rows, width = tokens.shape
    sub = rows // n_tp
    piece = width // n_ep
    half = width // 2
    local_experts, _, _ = gate_weight.shape
    experts = local_experts * n_ep
    scale = HEAD_SIZE ** (-0.5)
    q_cols = query_weight.shape[1]
    k_cols = key_projection_matrix.shape[1]

    def own_rows(value):
        return lax.dynamic_slice_in_dim(value, tp_at * sub, sub, 0)

    def features(value, at):
        pieces = []
        for z in range(n_z):
            first = value[..., 2 * z * piece : (2 * z + 1) * piece]
            second = value[..., (2 * z + 1) * piece : (2 * z + 2) * piece]
            pieces.append(jnp.where(at == 0, first, second))
        return jnp.concatenate(pieces, axis=-1)

    def whole_features(own, other):
        pieces = []
        for z in range(n_z):
            mine = own[..., z * piece : (z + 1) * piece]
            theirs = other[..., z * piece : (z + 1) * piece]
            pieces += [jnp.where(x_at == 0, mine, theirs), jnp.where(x_at == 0, theirs, mine)]
        return jnp.concatenate(pieces, axis=-1)

    cols = q_cols + 2 * k_cols
    out_cols = out_weight.shape[1]
    packed = exchange(
        pack_weights(
            n_z, query_weight, key_projection_matrix, value_projection_matrix, out_weight,
            attn_gain, ffn_gain,
        ),
        "z",
    )
    other_tokens = flip(tokens, "x", 1)
    qkv_half = packed[:, :piece, :cols].reshape(half, cols)
    gain_half = packed[:, piece, cols : cols + piece].reshape(half).astype(f32)
    pair_tokens = jnp.concatenate([tokens, other_tokens], 0).astype(f32)
    pair_inverse = rms_inverse(pair_tokens)
    pair_normed = (features(pair_tokens, x_at) * pair_inverse * gain_half).astype(bf16)
    qkv_part = jnp.dot(pair_normed, qkv_half, preferred_element_type=f32)
    qkv = qkv_part[:rows] + flip(qkv_part[rows:].astype(bf16), "x", 1).astype(f32)

    out_own = packed[:, :, cols:]
    out_other = flip(out_own, "x", 1)
    out_packed = jnp.where(
        x_at == 0, jnp.stack([out_own, out_other], 1), jnp.stack([out_other, out_own], 1)
    )
    out_full = out_packed[:, :, :piece].reshape(width, out_cols)
    gain_one = out_packed[:, :, piece, :piece].reshape(width).astype(f32)
    gain_two = out_packed[:, :, piece + 1, :piece].reshape(width).astype(f32)

    expert_index = jnp.arange(experts, dtype=jnp.int32)
    own_ids = own_rows(route_ids)
    own_weights = own_rows(route_weights)
    dense = jnp.sum(
        jnp.where(own_ids[:, :, None] == expert_index, own_weights[:, :, None], 0.0), axis=1
    )
    dense = dense.reshape(sub, n_ep, local_experts).swapaxes(0, 1)
    dense_high, dense_low = split_pair(dense)
    dense_pack = jnp.concatenate([dense_high, dense_low], -1)
    dense_pack = dense_pack.reshape(n_z, 2, sub, 2 * local_experts)
    dense_pack = pad_to(jnp.concatenate([dense_pack[:, 0], dense_pack[:, 1]], -1), 2, LANES)
    cot_own = own_rows(cotangent)
    cot_pack = jnp.concatenate(
        [jnp.broadcast_to(cot_own[None], (n_z, sub, width)), dense_pack], axis=-1
    )
    cot_z = exchange(after(cot_pack, packed), "z")
    cot_x = flip(cot_z, "x", 1)
    cot_ep = jnp.where(x_at == 0, jnp.stack([cot_z, cot_x], 1), jnp.stack([cot_x, cot_z], 1))
    routed = cot_ep[..., width:]
    routed = jnp.where(
        x_at == 0, routed[..., : 2 * local_experts], routed[..., 2 * local_experts : 4 * local_experts]
    )
    cot_ep = jnp.concatenate([cot_ep[..., :width], pad_to(routed, 3, LANES)], axis=-1)
    cot_ep = cot_ep.reshape(n_ep * sub, width + LANES)

    position, allowed = positions_and_mask(segment_ids[0])
    cosine, sine = rope_tables(position)
    query = qkv[:, :q_cols].reshape(rows, -1, HEAD_SIZE)
    keys = qkv[:, q_cols : q_cols + k_cols].reshape(rows, -1, HEAD_SIZE)
    query_rot = rotate(query, cosine, sine).astype(bf16)
    key_rot = rotate(keys, cosine, sine).astype(bf16)
    value_rows = qkv[:, q_cols + k_cols :].astype(bf16).reshape(rows, -1, HEAD_SIZE)
    grouped = query_rot.reshape(rows, key_rot.shape[1], -1, HEAD_SIZE)
    scores = jnp.einsum("thgd,uhd->hgtu", grouped, key_rot, preferred_element_type=f32) * scale
    scores = jnp.where(allowed, scores, MASKED)
    peak = jnp.max(scores, axis=-1, keepdims=True)
    logsum = peak + jnp.log(jnp.sum(jnp.exp(scores - peak), axis=-1, keepdims=True))
    probs = jnp.exp(scores - logsum)
    probs_low = probs.astype(bf16)
    attended = jnp.einsum(
        "hgtu,uhd->thgd", probs_low, value_rows, preferred_element_type=f32
    ).astype(bf16)
    attended_flat = attended.reshape(rows, -1)
    branch_part = jnp.einsum("tk,dk->td", attended_flat, out_full, preferred_element_type=f32)
    branch = reduce_own(branch_part)
    tokens_own = own_rows(tokens).astype(f32)
    hidden_one = tokens_own + branch
    inverse_two = rms_inverse(hidden_one)
    normed_two = (hidden_one * inverse_two * gain_two).astype(bf16)

    rows_ep = gather_blocks(normed_two, EP).reshape(n_ep * sub, width)
    cot_parts = gather_offsets(cot_ep)
    row_parts = gather_offsets(rows_ep)
    offsets = sorted(row_parts)
    results = {}
    for k in offsets:
        cot_other = flip(cot_parts[k], "c", 1)
        row_other = flip(row_parts[k], "c", 1)
        parts = (row_parts[k], row_other, cot_parts[k], cot_other)
        results[k] = parts + tuple(run_experts(*parts, gate_weight, up_weight, down_weight))
    grad_c = {k: r[4] + flip(r[5], "c", 1).astype(f32) for k, r in results.items()}
    grad_c[0] = lax.optimization_barrier(grad_c[0])
    grad_y = reduce_offsets(dict(grad_c)).astype(bf16)
    moe_c = {}
    for k, r in results.items():
        moe = jnp.dot(r[6], down_weight.reshape(-1, width), preferred_element_type=f32)
        own_moe, other_moe = jnp.split(moe, 2)
        received = flip(other_moe.astype(bf16), "c", 1)
        moe_c[k] = own_moe + received.astype(f32)
    sent_moe = {k: v.astype(bf16) for k, v in moe_c.items() if k}
    for k, v in sent_moe.items():
        moe_c[k], grad_y = lax.optimization_barrier((v, grad_y))
    moe_y = reduce_offsets(moe_c).astype(bf16).reshape(n_ep, sub, width)
    grad_ep = exchange(grad_y.reshape(n_ep, sub, width), EP)
    ordered_results = [results[k] for k in offsets]
    gate_grad, up_grad, down_grad = run_grads(
        [part for r in ordered_results for part in r[:2]],
        [part for r in ordered_results for part in r[2:4]],
        *([r[i] for r in ordered_results] for i in (6, 7, 8)),
        local_experts,
    )
    grad_ep, gate_grad, up_grad, down_grad = lax.optimization_barrier(
        (grad_ep, gate_grad, up_grad, down_grad)
    )
    grad_normed_two = jnp.sum(grad_ep.astype(f32), axis=0)

    norm_term, ffn_gain_part = rms_backward(hidden_one, inverse_two, gain_two, grad_normed_two)
    grad_hidden_one = cot_own.astype(f32) + norm_term
    ffn_rows = pad_to(jnp.stack(split_pair(ffn_gain_part)), 0, SUBLANES)
    branch_rows = lax.all_gather(
        jnp.concatenate([grad_hidden_one.astype(bf16), ffn_rows], 0), TP, axis=0
    )
    grad_branch = branch_rows[:, :sub].reshape(rows, width)
    ffn_gain_part = jnp.sum(branch_rows[:, sub : sub + 2].astype(f32), axis=(0, 1))

    attended_other = flip(after(attended_flat, normed_two), "x", 1)
    branch_other = flip(features(grad_branch, 1 - x_at), "x", 1)
    branch_half = features(grad_branch, x_at)
    out_part = jnp.einsum(
        "td,tk->dk",
        jnp.concatenate([branch_half, branch_other], 0),
        jnp.concatenate([attended_flat, attended_other], 0),
        preferred_element_type=f32,
    )

    grad_attended = jnp.dot(grad_branch, out_full, preferred_element_type=f32)
    grad_attended = grad_attended.astype(bf16).reshape(attended.shape)
    value_grad = jnp.einsum("hgtu,thgd->uhd", probs_low, grad_attended, preferred_element_type=f32)
    grad_probs = jnp.einsum("thgd,uhd->hgtu", grad_attended, value_rows, preferred_element_type=f32)
    delta = jnp.einsum("thgd,thgd->hgt", grad_attended, attended, preferred_element_type=f32)
    grad_scores = (probs * (grad_probs - delta[..., None]) * scale).astype(bf16)
    query_grad_rot = jnp.einsum("hgtu,uhd->thgd", grad_scores, key_rot, preferred_element_type=f32)
    key_grad_rot = jnp.einsum("hgtu,thgd->uhd", grad_scores, grouped, preferred_element_type=f32)
    query_back = rotate_back(query_grad_rot.reshape(rows, -1, HEAD_SIZE), cosine, sine)
    key_back = rotate_back(key_grad_rot, cosine, sine)
    qkv_grad = jnp.concatenate(
        [
            query_back.reshape(rows, -1).astype(bf16),
            key_back.reshape(rows, -1).astype(bf16),
            value_grad.reshape(rows, -1).astype(bf16),
        ],
        axis=1,
    )

    qkv_grad_other = flip(qkv_grad, "x", 1)
    qkv_part = jnp.einsum(
        "td,tk->dk",
        pair_normed,
        jnp.concatenate([qkv_grad, qkv_grad_other], 0),
        preferred_element_type=f32,
    )
    grad_part = jnp.concatenate([qkv_part, out_part], 1).astype(bf16)
    grad_blocks = exchange(grad_part.reshape(n_z, piece, cols + out_cols), "z")

    def block_sum(start, size):
        return jnp.sum(grad_blocks[:, :, start : start + size].astype(f32), axis=0)

    qkv_other_half = flip(after(qkv_half, rows_ep), "x", 1)
    normed_part = whole_features(
        jnp.einsum("tk,dk->td", qkv_grad, qkv_half, preferred_element_type=f32),
        jnp.einsum("tk,dk->td", qkv_grad, qkv_other_half, preferred_element_type=f32),
    )
    grad_normed_one = reduce_own(normed_part)
    input_term, attn_gain_part = rms_backward(
        tokens_own, own_rows(pair_inverse[:rows]), gain_one, grad_normed_one
    )
    attn_rows = pad_to(jnp.stack(split_pair(attn_gain_part)), 0, SUBLANES)
    moe_ep = exchange(after(moe_y, grad_ep), EP)
    moe_own = jnp.sum(moe_ep.astype(f32), axis=0)
    mixed_own = (hidden_one + moe_own).astype(bf16)
    last_rows = lax.all_gather(
        jnp.concatenate(
            [(grad_hidden_one + input_term).astype(bf16), mixed_own, attn_rows], 0
        ),
        TP,
        axis=0,
    )
    tokens_grad = last_rows[:, :sub].reshape(rows, width).astype(f32)
    mixed = last_rows[:, sub : 2 * sub].reshape(rows, width)
    gain_sum = jnp.sum(last_rows[:, 2 * sub : 2 * sub + 2].astype(f32), axis=(0, 1))
    gain_sum = jnp.stack([gain_sum, ffn_gain_part]).reshape(2, -1, LANES)
    gain_sum = gain_sum + flip(gain_sum, "x", 1)
    for bit in bits_of("z"):
        gain_sum = gain_sum + flip(gain_sum, "z", bit)
    both_gains = lax.dynamic_slice_in_dim(
        gain_sum.reshape(2, width), lax.axis_index(EP) * piece, piece, 1
    )
    attn_gain_grad, ffn_gain_grad = both_gains[0], both_gains[1]
    return (
        mixed,
        tokens_grad,
        attn_gain_grad,
        block_sum(0, q_cols),
        block_sum(q_cols, k_cols),
        block_sum(q_cols + k_cols, k_cols),
        block_sum(cols, out_cols),
        ffn_gain_grad,
        gate_grad,
        up_grad,
        down_grad,
    )


def solution(mesh):
    n_ep, n_tp = mesh.devices.shape
    split = jax.sharding.Mesh(
        mesh.devices.reshape(n_ep // 2, 2, n_tp // 2, 2), ("z", "x", "y", "c")
    )
    return jax.shard_map(
        body,
        mesh=split,
        in_specs=(
            P(EP, None),
            P(EP, None),
            P(EP, None),
            P(EP, None),
            P(EP),
            P(EP, TP),
            P(EP, TP),
            P(EP, TP),
            P(EP, TP),
            P(EP),
            P(EP, None, TP),
            P(EP, None, TP),
            P(EP, TP, None),
            P(EP, None),
        ),
        out_specs=(
            P(EP, None),
            P(EP, None),
            P(EP),
            P(EP, TP),
            P(EP, TP),
            P(EP, TP),
            P(EP, TP),
            P(EP),
            P(EP, None, TP),
            P(EP, None, TP),
            P(EP, TP, None),
        ),
        check_vma=False,
    )
```
